256 devices in a mesh: dp: 16 (over y, x), tensor: 8 (over z), layers: 2 (over core).
Axes of the slice: x: 4, y: 4, z: 8, core: 2. Of those that a mesh axis runs over, the one named last changes fastest.
Arguments:
- section_input: bfloat16 [2, 2048, 4096], P('layers', 'dp', 'tensor'), may hold values from -24 to 24
- out_cotangent: bfloat16 [2048, 4096], P('dp', 'tensor'), may hold values from -24 to 24
- lift_weight: bfloat16 [2, 2048, 4096], P('layers', None, 'tensor'), may hold values from -0.125 to 0.125
- proj_weight: bfloat16 [2, 4096, 4096], P('layers', None, 'tensor'), may hold values from -0.09375 to 0.09375
- lift_mask: int32 [2, 16, 32], P('layers', None, 'tensor'), may hold values 0 or 1
- proj_mask: int32 [2, 32, 32], P('layers', None, 'tensor'), may hold values 0 or 1
- channel_perm: int32 [2, 4096], P('layers'), may hold values from 0 to 4095, each once within a row
- lift_moment: float32 [2, 2048, 4096], P('layers', 'dp', 'tensor'), may hold values from -3 to 3
- lift_square: float32 [2, 2048, 4096], P('layers', 'dp', 'tensor'), may hold values from 0.25 to 1
- proj_moment: float32 [2, 4096, 4096], P('layers', 'dp', 'tensor'), may hold values from -3 to 3
- proj_square: float32 [2, 4096, 4096], P('layers', 'dp', 'tensor'), may hold values from 0.25 to 1
Outputs:
- input_grad: float32 [2, 2048, 4096], P('layers', 'dp', 'tensor')
- log_det: float32 [2], P('layers')
- lift_first: float32 [2, 2048, 4096], P('layers', 'dp', 'tensor')
- lift_second: float32 [2, 2048, 4096], P('layers', 'dp', 'tensor')
- lift_update: float32 [2, 2048, 4096], P('layers', 'dp', 'tensor')
- proj_first: float32 [2, 4096, 4096], P('layers', 'dp', 'tensor')
- proj_second: float32 [2, 4096, 4096], P('layers', 'dp', 'tensor')
- proj_update: float32 [2, 4096, 4096], P('layers', 'dp', 'tensor')
The draws below stay inside these ranges and needn't reach their ends.
Inputs may be any that keep to these rules, and one draw needn't show every extreme that they name: `channel_perm`: each row orders all 4096 features once. `lift_mask`: 1 keeps a block of 128 x 128 weights, 0 prunes it. `proj_mask`: 1 keeps a block of 128 x 128 weights, 0 prunes it.
All inputs are finite; a program needn't handle non-finite values.
Results may differ from the reference program's by a relative error of at most 0.008.
Values may be sent and summed in bfloat16 or wider, within the bound.
A program may use at most 128 MiB of HBM per device.

```python
import jax
import jax.numpy as jnp
from jax import lax

FEAT = 4096
HID = 4096
BLK = 128
ADAM_STEP = 10
HALF = 2048
TOKENS = 2048
CLIP = 4096
N_TENSOR = 8


def draw_out_cotangent(key, part):
    row_key, base_key = jax.random.split(key, 2)
    row_scale = jnp.exp(jax.random.uniform(row_key, (TOKENS, 1), jnp.float32, jnp.log(0.3), jnp.log(3.0)))
    col_scale = 0.6 * jnp.power(3.0, jnp.arange(FEAT, dtype=jnp.float32) / FEAT)[None, :]
    base_draw = jnp.clip(jax.random.normal(base_key, (TOKENS, FEAT), jnp.float32), -4.0, 4.0)
    return (row_scale * col_scale * base_draw).astype(jnp.bfloat16)


def draw_section_input(key, part):
    inner_key = jax.random.fold_in(key, 7)
    base_key = jax.random.fold_in(inner_key, 0)
    position = jnp.arange(TOKENS, dtype=jnp.float32)[None, :, None] / TOKENS
    row_scale = 0.3 * jnp.power(20.0, position)
    base_draw = jnp.clip(jax.random.normal(base_key, (2, TOKENS, FEAT), jnp.float32), -3.9, 3.9)
    return (row_scale * base_draw).astype(jnp.bfloat16)


def touch_ends(result, own_key, smallest, high):
    extent = result.shape
    index_at = [jax.random.randint(jax.random.fold_in(own_key, axis), (), 0, extent[axis]) for axis in range(len(extent))]
    result = result.at[tuple(index_at)].set(smallest)
    longest = extent.index(max(extent))
    index_at[longest] = (index_at[longest] + 1) % extent[longest]
    return result.at[tuple(index_at)].set(high)


def levels(key, dims, cuts, smallest, top_value):
    def one(dim, parts):
        heights = jax.random.uniform(jax.random.fold_in(jax.random.fold_in(key, 6), dim), (parts,), jnp.float32, smallest / len(cuts), top_value / len(cuts))
        return jnp.repeat(jnp.exp(heights), dims[dim] // parts).reshape((-1,) + (1,) * (len(dims) - dim - 1))

    factor_of = one(*cuts[0])
    for cut in cuts[1:]:
        factor_of = factor_of * one(*cut)
    return factor_of


def gaussian(rng, extent, scale, reach, pieces=(), held_as=jnp.bfloat16):
    loudness = levels(rng, extent, pieces, -0.22, 0.18) if pieces else 1.0
    entries = jax.random.normal(rng, extent, jnp.float32) * scale * loudness
    return jnp.minimum(jnp.maximum(entries, -reach), reach).astype(held_as)


def setup_inputs(seed: int = 0) -> dict:
    streams_of = jax.random.split(jax.random.key(seed), 12)
    return {
        "section_input": draw_section_input(jax.random.fold_in(streams_of[11], 71), 0),
        "out_cotangent": draw_out_cotangent(jax.random.fold_in(streams_of[11], 71), 0),
        "lift_weight": gaussian(streams_of[2], (2, HALF, HID), HALF ** -0.5, 0.125, ((0, 2), (2, 8))),
        "proj_weight": gaussian(streams_of[3], (2, 2 * HALF, HID), HID ** -0.5, 0.09375, ((0, 2), (2, 8))),
        "lift_mask": touch_ends((jax.random.randint(streams_of[4], (2, HALF // BLK, HID // BLK), 0, 2) < 1).astype(jnp.int32), jax.random.fold_in(streams_of[4], 1), 0, 1),
        "proj_mask": touch_ends((jax.random.randint(streams_of[5], (2, 2 * HALF // BLK, HID // BLK), 0, 2) < 1).astype(jnp.int32), jax.random.fold_in(streams_of[5], 1), 0, 1),
        "channel_perm": jax.vmap(lambda own: jax.random.permutation(own, FEAT))(jax.random.split(streams_of[6], 2)).reshape((2, FEAT)).astype(jnp.int32),
        "lift_moment": gaussian(streams_of[7], (2, HALF, HID), 0.5, 3.0, ((0, 2), (1, 16), (2, 8)), jnp.float32),
        "lift_square": jnp.clip(0.25 + 0.75 * jax.random.uniform(streams_of[8], (2, HALF, HID), jnp.float32) ** levels(streams_of[8], (2, HALF, HID), ((0, 2), (1, 16), (2, 8)), -0.2, 0.2), 0.25, 1.0),
        "proj_moment": gaussian(streams_of[9], (2, 2 * HALF, HID), 0.5, 3.0, ((0, 2), (1, 16), (2, 8)), jnp.float32),
        "proj_square": jnp.clip(0.25 + 0.75 * jax.random.uniform(streams_of[10], (2, 2 * HALF, HID), jnp.float32) ** levels(streams_of[10], (2, 2 * HALF, HID), ((0, 2), (1, 16), (2, 8)), -0.2, 0.2), 0.25, 1.0),
    }


beta_one = 0.9
beta_two = 0.99
adam_eps = 1e-08

def expand_blocks(block_mask):
    return jnp.repeat(jnp.repeat(block_mask, BLK, axis=0), BLK, axis=1) > 0

def shard_sum(left_mat, right_mat):
    part_width = left_mat.shape[1] // N_TENSOR
    running = jnp.zeros((left_mat.shape[0], right_mat.shape[0]), jnp.float32)
    for shard_idx in range(N_TENSOR):
        lo_col = shard_idx * part_width
        piece_sum = jnp.dot(left_mat[:, lo_col:lo_col + part_width], right_mat[:, lo_col:lo_col + part_width].T, preferred_element_type=jnp.float32)
        running = running + lax.optimization_barrier(piece_sum.astype(jnp.bfloat16)).astype(jnp.float32)
    return running

def section_grads(tokens, cotangent, lift_eff, proj_eff, channel_order):
    permuted = tokens[:, channel_order]
    cond_side = permuted[:, :HALF]
    moved_side = permuted[:, HALF:].astype(jnp.float32)
    pre_act = jnp.dot(cond_side, lift_eff, preferred_element_type=jnp.float32)
    hidden = jax.nn.silu(pre_act).astype(jnp.bfloat16)
    shared = shard_sum(hidden, proj_eff)
    raw_scale = shared[:, :HALF]
    shift_term = shared[:, HALF:]
    scale_term = jax.nn.sigmoid(raw_scale + 2.0)
    keep_part = 1.0 - scale_term
    log_mean = jnp.sum(jax.nn.log_sigmoid(raw_scale + 2.0)) / (TOKENS * HALF)
    grad_cond = cotangent[:, :HALF]
    grad_moved = cotangent[:, HALF:]
    grad_raw = grad_moved * (moved_side + shift_term) * scale_term * keep_part - keep_part
    grad_shift = grad_moved * scale_term
    grad_st = jnp.concatenate([grad_raw, grad_shift], axis=1).astype(jnp.bfloat16)
    grad_act = jnp.dot(grad_st, proj_eff, preferred_element_type=jnp.float32)
    squash = jax.nn.sigmoid(pre_act)
    grad_pre = (grad_act * squash * (1.0 + pre_act * (1.0 - squash))).astype(jnp.bfloat16)
    grad_inputs = grad_cond + shard_sum(grad_pre, lift_eff)
    grad_mixed = jnp.concatenate([grad_inputs, grad_shift], axis=1)
    inverse = jnp.zeros((FEAT,), jnp.int32).at[channel_order].set(jnp.arange(FEAT, dtype=jnp.int32))
    grad_in = grad_mixed[:, inverse]
    lift_grad = jnp.dot(cond_side.T, grad_pre, preferred_element_type=jnp.float32)
    proj_grad = jnp.dot(grad_st.T, hidden, preferred_element_type=jnp.float32)
    return (grad_in, log_mean, lift_grad, proj_grad)

def adam_step(gradient, kept, moment, square, factor):
    scaled = gradient * factor
    new_first = jnp.where(kept, beta_one * moment + (1.0 - beta_one) * scaled, moment)
    new_second = jnp.where(kept, beta_two * square + (1.0 - beta_two) * scaled * scaled, square)
    bias_one = 1.0 - beta_one ** ADAM_STEP
    bias_two = 1.0 - beta_two ** ADAM_STEP
    update = jnp.where(kept, new_first / bias_one / (jnp.sqrt(new_second / bias_two) + adam_eps), 0.0)
    return (new_first, new_second, update)

def reference(section_input, out_cotangent, lift_weight, proj_weight, lift_mask, proj_mask, channel_perm, lift_moment, lift_square, proj_moment, proj_square):
    cotangent = out_cotangent.astype(jnp.float32)
    grad_list = [None, None]
    log_list = [None, None]
    lift_grads = [None, None]
    proj_grads = [None, None]
    lift_keeps = [None, None]
    proj_keeps = [None, None]
    for section_idx in (1, 0):
        lift_keep = expand_blocks(lift_mask[section_idx])
        proj_keep = expand_blocks(proj_mask[section_idx])
        lift_eff = jnp.where(lift_keep, lift_weight[section_idx], jnp.zeros((), jnp.bfloat16))
        proj_eff = jnp.where(proj_keep, proj_weight[section_idx], jnp.zeros((), jnp.bfloat16))
        grad_in, log_mean, lift_grad, proj_grad = section_grads(section_input[section_idx], cotangent, lift_eff, proj_eff, channel_perm[section_idx])
        grad_list[section_idx] = grad_in
        log_list[section_idx] = log_mean
        lift_grads[section_idx] = jnp.where(lift_keep, lift_grad, 0.0)
        proj_grads[section_idx] = jnp.where(proj_keep, proj_grad, 0.0)
        lift_keeps[section_idx] = lift_keep
        proj_keeps[section_idx] = proj_keep
        cotangent = lax.optimization_barrier(grad_in.astype(jnp.bfloat16)).astype(jnp.float32)
    square_total = jnp.float32(0.0)
    for section_idx in (0, 1):
        square_total = square_total + jnp.sum(lift_grads[section_idx] * lift_grads[section_idx]) + jnp.sum(proj_grads[section_idx] * proj_grads[section_idx])
    factor = jnp.minimum(1.0, CLIP / (jnp.sqrt(square_total) + 1e-06))
    lift_out = [adam_step(lift_grads[s], lift_keeps[s], lift_moment[s], lift_square[s], factor) for s in (0, 1)]
    proj_out = [adam_step(proj_grads[s], proj_keeps[s], proj_moment[s], proj_square[s], factor) for s in (0, 1)]
    input_grad = jnp.stack(grad_list)
    log_det = jnp.stack(log_list)
    return (input_grad, log_det, jnp.stack([lift_out[0][0], lift_out[1][0]]), jnp.stack([lift_out[0][1], lift_out[1][1]]), jnp.stack([lift_out[0][2], lift_out[1][2]]), jnp.stack([proj_out[0][0], proj_out[1][0]]), jnp.stack([proj_out[0][1], proj_out[1][1]]), jnp.stack([proj_out[0][2], proj_out[1][2]]))
```

```python
import jax
import jax.numpy as jnp
from jax import lax
from jax.experimental import pallas as pl
from jax.experimental.pallas import tpu as pltpu
from jax.sharding import Mesh
from jax.sharding import PartitionSpec as P

BLK = 128
ADAM_STEP = 10
CLIP = 4096
DP = ("dp_0", "dp_1")
MESH = pl.DeviceIdType.MESH
F32 = jnp.float32
BF16 = jnp.bfloat16

NZ = 8
NR = 4

beta_one = 0.9
beta_two = 0.99
adam_eps = 1e-08


def nn(a, b):
    return jnp.dot(a, b, preferred_element_type=F32)


def nt(a, b):
    return lax.dot_general(a, b, (((1,), (1,)), ((), ())), preferred_element_type=F32)


def tn(a, b):
    return lax.dot_general(a, b, (((0,), (0,)), ((), ())), preferred_element_type=F32)


def al(i, m):
    return pl.multiple_of(i, m)


def remote(src, dst, ssem, rsem, **where):
    return pltpu.make_async_remote_copy(
        src_ref=src, dst_ref=dst, send_sem=ssem, recv_sem=rsem, device_id=where, device_id_type=MESH
    )


def both_ways(d, s, h):
    return s < 3 or d == h


def token_kernel(
    x_ref,
    cot_ref,
    lift_ref,
    proj_ref,
    lmask_ref,
    pmask_ref,
    perm_ref,
    gin_ref,
    logp_ref,
    condc_ref,
    stc_ref,
    hid_ref,
    gp_ref,
    xbuf,
    pc,
    m,
    lift,
    proj,
    acc,
    cond,
    moved,
    slope,
    pre,
    stbuf,
    sbuf,
    rbuf,
    cbuf,
    c0buf,
    gbuf,
    cown,
    ag_s,
    ag_r,
    rs_s,
    rs_r,
    cs,
    cr,
    gs,
    gr,
    hs,
    hr,
    a_s,
    a_r,
    ts,
    tr,
    xs,
    xr,
):
    z = lax.axis_index("tensor")
    y = lax.axis_index("dp_0")
    x = lax.axis_index("dp_1")
    core = lax.axis_index("layers")
    me = y * NR + x
    tok = x_ref.shape[0]
    half = tok // 2
    quart = tok // 4
    w = x_ref.shape[1]
    q = w // 2
    hw = NZ * q

    def rows(h):
        return pl.ds(h * half, half)

    def zr(i):
        return lax.rem(z + NZ + i, NZ)

    zside = (zr(1), zr(-1))

    bar = pltpu.get_barrier_semaphore()
    for i in range(1, NZ):
        pl.semaphore_signal(bar, inc=1, device_id={"tensor": zr(i)}, device_id_type=MESH)
    for oy in range(NR):
        for ox in range(NR):
            if oy or ox:
                pl.semaphore_signal(
                    bar,
                    inc=1,
                    device_id={"dp_0": lax.rem(y + oy, NR), "dp_1": lax.rem(x + ox, NR)},
                    device_id_type=MESH,
                )
    pl.semaphore_signal(bar, inc=1, device_id={"layers": 1 - core}, device_id_type=MESH)
    pl.semaphore_wait(bar, NZ - 1 + NR * NR - 1 + 1)

    def ag_copy(p, buf, own, s, d, h):
        origin = zr(-s) if d == 0 else zr(s)
        src = own.at[rows(h)] if s == 0 else buf.at[origin, rows(h)]
        return remote(src, buf.at[origin, rows(h)], ag_s.at[p, d, s, h], ag_r.at[p, d, s, h], tensor=zside[d])

    def ag_wait(p, buf, s, d, h):
        origin = zr(-1 - s) if d == 0 else zr(1 + s)
        ref = buf.at[origin, rows(h)]
        remote(ref, ref, ag_s.at[p, d, s, h], ag_r.at[p, d, s, h], tensor=zside[d]).wait_recv()

    def ag_start(p, buf, own):
        for d in (0, 1):
            for h in (d, 1 - d):
                ag_copy(p, buf, own, 0, d, h).start()

    def ag_step(p, buf, own, s):
        for k in (0, 1):
            for d in (0, 1):
                h = d if k == 0 else 1 - d
                if both_ways(d, s, h):
                    ag_wait(p, buf, s, d, h)
                    if s < 3 and both_ways(d, s + 1, h):
                        ag_copy(p, buf, own, s + 1, d, h).start()
        return [zr(-1 - s), zr(1 + s)] if s < 3 else [zr(4)]

    def ag_finish(p, buf, own):
        for d in (0, 1):
            for s in range(4):
                for h in (0, 1):
                    if both_ways(d, s, h):
                        ag_copy(p, buf, own, s, d, h).wait_send()

    def rs_copy(p, s, d, h):
        return remote(
            sbuf.at[p, d, s, rows(h)],
            rbuf.at[p, d, s, rows(h)],
            rs_s.at[p, d, s, h],
            rs_r.at[p, d, s, h],
            tensor=zside[d],
        )

    def rs(p, part, tick):
        far = part(zr(4))
        for d in (0, 1):
            sbuf[p, d, 0, rows(d)] = far[d * half : (d + 1) * half].astype(BF16)
            rs_copy(p, 0, d, d).start()
        for s in (1, 2, 3):
            mine = [part(zr(4 - s)), part(zr(s - 4))]
            for k in (0, 1):
                for d in (0, 1):
                    h = (1 - d if s == 1 else d) if k == 0 else (d if s == 1 else 1 - d)
                    own = mine[d][h * half : (h + 1) * half]
                    if s > 1 or h == d:
                        rs_copy(p, s - 1, d, h).wait_recv()
                        own = own + rbuf[p, d, s - 1, rows(h)].astype(F32)
                    sbuf[p, d, s, rows(h)] = own.astype(BF16)
                    rs_copy(p, s, d, h).start()
            tick(s)
        own = part(z)
        for d in (0, 1):
            for h in (0, 1):
                rs_copy(p, 3, d, h).wait_recv()
        return own + rbuf[p, 0, 3].astype(F32) + rbuf[p, 1, 3].astype(F32)

    def rs_finish(p):
        for d in (0, 1):
            for s in range(4):
                for h in (0, 1):
                    if s > 0 or h == d:
                        rs_copy(p, s, d, h).wait_send()

    def along(axis, i):
        if axis == "dp_1":
            return {"dp_1": lax.rem(x + NR + i, NR)}
        return {"dp_0": lax.rem(y + NR + i, NR)}

    def slot(buf, stage, h, off, r):
        axis = ("dp_1", "dp_0")[(h + stage) % 2]
        yy, xx = (y, lax.rem(x + NR + off, NR)) if axis == "dp_1" else (lax.rem(y + NR + off, NR), x)
        if stage == 0:
            return buf.at[yy, xx, r]
        return buf.at[yy, :, r] if axis == "dp_0" else buf.at[:, xx, r]

    def xy_rows(h, t, d):
        if t == 0:
            return rows(h)
        return pl.ds(h * half + d * quart, quart)

    def xy_copy(p, buf, stage, h, t, d):
        axis = ("dp_1", "dp_0")[(h + stage) % 2]
        step = 1 if d == 0 else -1
        src = slot(buf, stage, h, 0 if t == 0 else -step, xy_rows(h, t, d))
        return remote(
            src, src, xs.at[p, stage, h, t, d], xr.at[p, stage, h, t, d], **along(axis, step)
        )

    def xy_wait(p, buf, stage, h, t, d):
        axis = ("dp_1", "dp_0")[(h + stage) % 2]
        step = 1 if d == 0 else -1
        ref = slot(buf, stage, h, -step if t == 0 else -2 * step, xy_rows(h, t, d))
        remote(
            ref, ref, xs.at[p, stage, h, t, d], xr.at[p, stage, h, t, d], **along(axis, step)
        ).wait_recv()

    def xy_tick(p, buf, k):
        stage, t = k // 2, k % 2
        if k:
            ps, pt = (k - 1) // 2, (k - 1) % 2
            for h in (0, 1):
                for d in (0, 1):
                    xy_wait(p, buf, ps, h, pt, d)
        if k < 4:
            for h in (0, 1):
                for d in (0, 1):
                    xy_copy(p, buf, stage, h, t, d).start()

    def xy_finish(p, buf):
        for stage in (0, 1):
            for h in (0, 1):
                for t in (0, 1):
                    for d in (0, 1):
                        xy_copy(p, buf, stage, h, t, d).wait_send()

    ag_start(0, xbuf, x_ref)

    @pl.when(core == 1)
    def _():
        for e in (0, 1):
            dest = lax.rem(2 * z + e, NZ)
            piece = cot_ref.at[:, pl.ds(e * q, q)]
            land = cbuf.at[:, pl.ds(al((z // 4) * q, q), q)]

            @pl.when(dest != z)
            def _():
                remote(piece, land, cs.at[e], cr.at[z // 4], tensor=dest).start()

            @pl.when(dest == z)
            def _():
                cbuf[:, pl.ds(al((z // 4) * q, q), q)] = cot_ref[:, pl.ds(e * q, q)]

    def mask_rows(i, _):
        r = pl.ds(al(i * BLK, BLK), BLK)
        for c in range(w // BLK):
            cc = pl.ds(c * BLK, BLK)
            keep = lmask_ref[i, c].astype(F32)
            lift[r, cc] = (lift_ref[r, cc].astype(F32) * keep).astype(BF16)
        return 0

    def mask_rows_proj(i, _):
        r = pl.ds(al(i * BLK, BLK), BLK)
        for c in range(w // BLK):
            cc = pl.ds(c * BLK, BLK)
            keep = pmask_ref[i, c].astype(F32)
            proj[r, cc] = (proj_ref[r, cc].astype(F32) * keep).astype(BF16)
        return 0

    ca_perm = pl.ds(al(z * q, q), q)
    mv_perm = pl.ds(al(hw + z * q, q), q)

    def hot(base, order):
        at = lax.broadcasted_iota(jnp.int32, (BLK, q), 0) + base
        return jnp.where(at == order, 1.0, 0.0).astype(BF16)

    def build(origin):
        def body(i, _):
            base = origin * w + i * BLK
            r = pl.ds(al(base, BLK), BLK)
            for c in range(hw // q):
                cc = pl.ds(c * q, q)
                pc[r, cc] = hot(base, perm_ref[:, cc])
            m[r, pl.ds(w, q)] = hot(base, perm_ref[:, ca_perm])
            m[r, pl.ds(w + q, q)] = hot(base, perm_ref[:, mv_perm])
            return 0

        lax.fori_loop(0, w // BLK, body, 0)

    def pick(origin, first, src):
        r = pl.ds(al(origin * w, w), w)
        block = src[...]

        def body(c, _):
            cc = pl.ds(al(c * q, q), q)
            got = nn(block, pc[r, cc])
            if first:
                acc[:, cc] = got
            else:
                acc[:, cc] += got
            return 0

        lax.fori_loop(0, hw // q, body, 0)
        got = nn(block, m[r, pl.ds(w + q, q)])
        if first:
            moved[...] = got
        else:
            moved[...] += got

    lax.fori_loop(0, hw // BLK, mask_rows, 0)
    build(z)
    pick(z, True, x_ref)
    build(zr(-1))
    build(zr(1))
    for s in range(4):
        came = ag_step(0, xbuf, x_ref, s)
        if s == 0:
            lax.fori_loop(0, 2 * hw // BLK, mask_rows_proj, 0)
        if s < 2:
            build(zr(-2 - s))
            build(zr(2 + s))
        elif s == 2:
            build(zr(4))
        for origin in came:
            pick(origin, False, xbuf.at[origin])
    cond[...] = acc[...].astype(BF16)

    pre[...] = nn(cond[...], lift[...])
    squash = jax.nn.sigmoid(pre[...])
    slope[...] = squash * (1.0 + pre[...] * (1.0 - squash))
    hid_ref[y, x] = (pre[...] * squash).astype(BF16)
    xy_tick(0, hid_ref, 0)

    def cond_copy(o):
        oy, ox = o // NR, o % NR
        ty, tx = lax.rem(y + oy, NR), lax.rem(x + ox, NR)
        return remote(
            cond.at[:, pl.ds(al((ty * NR + tx) * BLK, BLK), BLK)],
            condc_ref.at[me],
            a_s.at[o],
            a_r.at[o],
            dp_0=ty,
            dp_1=tx,
        )

    def cond_wait(o):
        oy, ox = o // NR, o % NR
        fy, fx = lax.rem(y + NR - oy, NR), lax.rem(x + NR - ox, NR)
        ref = condc_ref.at[fy * NR + fx]
        remote(ref, ref, a_s.at[o], a_r.at[o], dp_0=fy, dp_1=fx).wait_recv()

    for o in range(1, NR * NR):
        cond_copy(o).start()
    condc_ref[me] = cond[:, pl.ds(al(me * BLK, BLK), BLK)]

    hidden = hid_ref[y, x]

    def proj_rows(d, k):
        return pl.ds(al(k * hw + d * q, q), q)

    def shared_part(d):
        return jnp.concatenate(
            [nt(hidden, proj[proj_rows(d, 0), :]), nt(hidden, proj[proj_rows(d, 1), :])], axis=1
        )

    def spread(i):
        r = pl.ds(al(i * w, w), w)
        m[r, pl.ds(0, w)] = nn(pc[r, :], lift[...]).astype(BF16)

    def shared_tick(s):
        spread(s - 1)

    shared = rs(0, shared_part, shared_tick)
    xy_tick(0, hid_ref, 1)
    raw = shared[:, :q] + 2.0
    shift = shared[:, q:]
    scale = jax.nn.sigmoid(raw)
    keep_part = 1.0 - scale
    logs = jnp.minimum(raw, 0.0) - jnp.log1p(jnp.exp(-jnp.abs(raw)))
    logp_ref[...] = jnp.sum(logs.reshape(tok // 8, 8, q), axis=0)
    acc[:, pl.ds(0, q)] = scale
    acc[:, pl.ds(q, q)] = moved[...] + shift
    spread(3)
    xy_tick(0, hid_ref, 2)

    @pl.when(core == 1)
    def _():
        for k in (0, 1):

            @pl.when(4 * k + z // 2 != z)
            def _():
                ref = cbuf.at[:, pl.ds(k * q, q)]
                remote(ref, ref, cs.at[0], cr.at[k], tensor=z).wait_recv()

        cown[...] = cbuf[...]

    def hand():
        return remote(c0buf, c0buf, hs, hr, layers=1 - core)

    def gsend(k):
        dest = 4 * k + z // 2
        return remote(
            cown.at[:, pl.ds(k * q, q)],
            gbuf.at[:, pl.ds(al(lax.rem(z, 2) * q, q), q)],
            gs.at[k],
            gr.at[lax.rem(z, 2)],
            tensor=dest,
        )

    @pl.when(core == 0)
    def _():
        remote(gbuf, c0buf, hs, hr, layers=1 - core).wait_recv()
        cown[...] = c0buf[...]

    ca = cown[:, pl.ds(0, q)]
    cb = cown[:, pl.ds(q, q)].astype(F32)
    scale = acc[:, pl.ds(0, q)]
    keep_part = 1.0 - scale
    shift_grad = (cb * scale).astype(BF16)
    raw_grad = (cb * acc[:, pl.ds(q, q)] * scale * keep_part - keep_part).astype(BF16)
    stbuf[z, :, pl.ds(0, q)] = raw_grad
    stbuf[z, :, pl.ds(q, q)] = shift_grad
    own_st = stbuf.at[z]
    ag_start(1, stbuf, own_st)

    def st_piece(origin, k):
        return stbuf.at[origin, :, pl.ds(k * q, q)]

    def st_copy(origin, k):
        to = origin + NZ * k
        return remote(
            st_piece(origin, k), stc_ref.at[me], ts.at[to], tr.at[me], dp_0=to // NR, dp_1=lax.rem(to, NR)
        )

    def st_send(origin):
        for k in (0, 1):

            @pl.when(origin + NZ * k != me)
            def _():
                st_copy(origin, k).start()

            @pl.when(origin + NZ * k == me)
            def _():
                stc_ref[me] = stbuf[origin, :, pl.ds(k * q, q)]

    def act(origin):
        return nn(stbuf[origin, :, pl.ds(0, q)], proj[proj_rows(origin, 0), :]) + nn(
            stbuf[origin, :, pl.ds(q, q)], proj[proj_rows(origin, 1), :]
        )

    pre[...] = act(z)
    st_send(z)
    spread(4)
    for s in range(4):
        came = ag_step(1, stbuf, own_st, s)
        for origin in came:
            st_send(origin)
        if s < 3:
            spread(5 + s)
        for origin in came:
            pre[...] += act(origin)
        if s == 1:
            xy_tick(0, hid_ref, 3)
    grad_pre = (pre[...] * slope[...]).astype(BF16)
    gp_ref[y, x] = grad_pre
    xy_tick(0, hid_ref, 4)
    xy_tick(1, gp_ref, 0)

    lhs = jnp.concatenate([grad_pre, ca, shift_grad], axis=1)

    def in_rows(d, k):
        there = jnp.where(core == 1, k * hw + d * q, (2 * d + k) * q)
        return pl.ds(al(there, q), q)

    def in_part(d):
        return jnp.concatenate([nt(lhs, m[in_rows(d, 0), :]), nt(lhs, m[in_rows(d, 1), :])], axis=1)

    def in_tick(s):
        xy_tick(1, gp_ref, s)

    got = rs(1, in_part, in_tick)

    @pl.when(core == 1)
    def _():
        cown[...] = got.astype(BF16)
        remote(cown, c0buf, hs, hr, layers=1 - core).start()
        for k in (0, 1):

            @pl.when(4 * k + z // 2 != z)
            def _():
                gsend(k).start()

            @pl.when(4 * k + z // 2 == z)
            def _():
                gbuf[:, pl.ds(al(lax.rem(z, 2) * q, q), q)] = cown[:, pl.ds(k * q, q)]

    @pl.when(core == 0)
    def _():
        gin_ref[...] = got

    xy_tick(1, gp_ref, 4)

    @pl.when(core == 1)
    def _():
        for e in (0, 1):

            @pl.when(lax.rem(2 * z + e, NZ) != z)
            def _():
                ref = gbuf.at[:, pl.ds(e * q, q)]
                remote(ref, ref, gs.at[0], gr.at[e], tensor=z).wait_recv()

        gin_ref[...] = gbuf[...].astype(F32)
        remote(cown, c0buf, hs, hr, layers=1 - core).wait_send()
        for k in (0, 1):

            @pl.when(4 * k + z // 2 != z)
            def _():
                gsend(k).wait_send()

        for e in (0, 1):
            dest = lax.rem(2 * z + e, NZ)

            @pl.when(dest != z)
            def _():
                ref = cot_ref.at[:, pl.ds(e * q, q)]
                remote(ref, ref, cs.at[e], cr.at[0], tensor=dest).wait_send()

    for o in range(1, NR * NR):
        cond_wait(o)
        cond_copy(o).wait_send()

    def st_end(i, _):
        @pl.when(i != me)
        def _():
            ref = stc_ref.at[i]
            remote(ref, ref, ts.at[i], tr.at[i], dp_0=i // NR, dp_1=lax.rem(i, NR)).wait_recv()
            remote(ref, ref, ts.at[i], tr.at[i], dp_0=i // NR, dp_1=lax.rem(i, NR)).wait_send()

        return 0

    lax.fori_loop(0, NR * NR, st_end, 0)
    ag_finish(0, xbuf, x_ref)
    ag_finish(1, stbuf, own_st)
    rs_finish(0)
    rs_finish(1)
    xy_finish(0, hid_ref)
    xy_finish(1, gp_ref)


def token_side(x, cot, lift_w, proj_w, lmask, pmask, perm):
    tok, w = x.shape
    hw = lift_w.shape[0]
    feat = 2 * hw
    q = w // 2
    dma = pltpu.SemaphoreType.DMA
    vm = pl.BlockSpec(memory_space=pltpu.VMEM)
    sm = pl.BlockSpec(memory_space=pltpu.SMEM)
    n = NR * NR
    return pl.pallas_call(
        token_kernel,
        out_shape=(
            jax.ShapeDtypeStruct((tok, w), F32),
            jax.ShapeDtypeStruct((8, q), F32),
            jax.ShapeDtypeStruct((n, tok, BLK), BF16),
            jax.ShapeDtypeStruct((n, tok, q), BF16),
            jax.ShapeDtypeStruct((NR, NR, tok, w), BF16),
            jax.ShapeDtypeStruct((NR, NR, tok, w), BF16),
        ),
        in_specs=[vm, vm, vm, vm, sm, sm, vm],
        out_specs=(vm,) * 6,
        scratch_shapes=[
            pltpu.VMEM((NZ, tok, w), BF16),
            pltpu.VMEM((feat, hw), BF16),
            pltpu.VMEM((feat, 2 * w), BF16),
            pltpu.VMEM((hw, w), BF16),
            pltpu.VMEM((feat, w), BF16),
            pltpu.VMEM((tok, hw), F32),
            pltpu.VMEM((tok, hw), BF16),
            pltpu.VMEM((tok, q), F32),
            pltpu.VMEM((tok, w), F32),
            pltpu.VMEM((tok, w), F32),
            pltpu.VMEM((NZ, tok, w), BF16),
            pltpu.VMEM((2, 2, 4, tok, w), BF16),
            pltpu.VMEM((2, 2, 4, tok, w), BF16),
            pltpu.VMEM((tok, w), BF16),
            pltpu.VMEM((tok, w), BF16),
            pltpu.VMEM((tok, w), BF16),
            pltpu.VMEM((tok, w), BF16),
            dma((2, 2, 4, 2)),
            dma((2, 2, 4, 2)),
            dma((2, 2, 4, 2)),
            dma((2, 2, 4, 2)),
            dma((2,)),
            dma((2,)),
            dma((2,)),
            dma((2,)),
            dma,
            dma,
            dma((n,)),
            dma((n,)),
            dma((n,)),
            dma((n,)),
            dma((2, 2, 2, 2, 2)),
            dma((2, 2, 2, 2, 2)),
        ],
        compiler_params=pltpu.CompilerParams(
            collective_id=0, has_side_effects=True, vmem_limit_bytes=64 * 1024 * 1024 - 64 * 1024
        ),
        name="token_side",
    )(x, cot, lift_w, proj_w, lmask, pmask, perm)


def sum_kernel(v_ref, out_ref, zbuf, pbuf, mid, last, zs, zrv, ps, prv, ls, lr):
    z = lax.axis_index("tensor")
    y = lax.axis_index("dp_0")
    x = lax.axis_index("dp_1")
    core = lax.axis_index("layers")
    me = y * NR + x
    bar = pltpu.get_barrier_semaphore()
    for i in range(1, NZ):
        pl.semaphore_signal(bar, inc=1, device_id={"tensor": lax.rem(z + i, NZ)}, device_id_type=MESH)
    for o in range(1, NR * NR):
        ty, tx = lax.rem(y + o // NR, NR), lax.rem(x + o % NR, NR)
        pl.semaphore_signal(bar, inc=1, device_id={"dp_0": ty, "dp_1": tx}, device_id_type=MESH)
    pl.semaphore_signal(bar, inc=1, device_id={"layers": 1 - core}, device_id_type=MESH)
    pl.semaphore_wait(bar, NZ - 1 + NR * NR - 1 + 1)

    def zcopy(i):
        return remote(v_ref, zbuf.at[z], zs.at[i], zrv.at[i], tensor=lax.rem(z + i, NZ))

    for i in range(1, NZ):
        zcopy(i).start()
    zbuf[z] = v_ref[...]
    for i in range(1, NZ):
        ref = zbuf.at[lax.rem(z + NZ - i, NZ)]
        remote(ref, ref, zs.at[i], zrv.at[i], tensor=z).wait_recv()
    mid[...] = jnp.sum(zbuf[...], axis=0)

    def pcopy(o):
        ty, tx = lax.rem(y + o // NR, NR), lax.rem(x + o % NR, NR)
        return remote(mid, pbuf.at[me], ps.at[o], prv.at[o], dp_0=ty, dp_1=tx)

    for o in range(1, NR * NR):
        pcopy(o).start()
    pbuf[me] = mid[...]
    for o in range(1, NR * NR):
        fy, fx = lax.rem(y + NR - o // NR, NR), lax.rem(x + NR - o % NR, NR)
        ref = pbuf.at[fy * NR + fx]
        remote(ref, ref, ps.at[o], prv.at[o], dp_0=fy, dp_1=fx).wait_recv()
    last[0] = jnp.sum(pbuf[...], axis=0)
    swap = remote(last.at[0], last.at[1], ls, lr, layers=1 - core)
    swap.start()
    swap.wait_recv()
    out_ref[...] = last[0] + last[1]
    swap.wait_send()
    for i in range(1, NZ):
        zcopy(i).wait_send()
    for o in range(1, NR * NR):
        pcopy(o).wait_send()


def sum_all(v):
    dma = pltpu.SemaphoreType.DMA
    vm = pl.BlockSpec(memory_space=pltpu.VMEM)
    n = NR * NR
    return pl.pallas_call(
        sum_kernel,
        out_shape=jax.ShapeDtypeStruct(v.shape, F32),
        in_specs=[vm],
        out_specs=vm,
        scratch_shapes=[
            pltpu.VMEM((NZ,) + v.shape, F32),
            pltpu.VMEM((n,) + v.shape, F32),
            pltpu.VMEM(v.shape, F32),
            pltpu.VMEM((2,) + v.shape, F32),
            dma((NZ,)),
            dma((NZ,)),
            dma((n,)),
            dma((n,)),
            dma,
            dma,
        ],
        compiler_params=pltpu.CompilerParams(collective_id=1, has_side_effects=True),
        name="sum_all",
    )(v)


def expand_blocks(block_mask):
    blk_rows, blk_cols = block_mask.shape
    widened = jnp.broadcast_to((block_mask > 0)[:, None, :, None], (blk_rows, BLK, blk_cols, BLK))
    return widened.reshape(blk_rows * BLK, blk_cols * BLK)


def adam_step(gradient, kept, moment, square, factor):
    scaled = gradient * factor
    new_first = jnp.where(kept, beta_one * moment + (1.0 - beta_one) * scaled, moment)
    new_second = jnp.where(kept, beta_two * square + (1.0 - beta_two) * scaled * scaled, square)
    bias_one = 1.0 - beta_one**ADAM_STEP
    bias_two = 1.0 - beta_two**ADAM_STEP
    update = jnp.where(
        kept, new_first / bias_one / (jnp.sqrt(new_second / bias_two) + adam_eps), 0.0
    )
    return (new_first[None], new_second[None], update[None])


def per_device(
    section_input,
    out_cotangent,
    lift_weight,
    proj_weight,
    lift_mask,
    proj_mask,
    channel_perm,
    lift_moment,
    lift_square,
    proj_moment,
    proj_square,
):
    core = lax.axis_index("layers")
    dp_index = lax.axis_index(DP)
    gin, logp, condc, stc, hid, gp = token_side(
        section_input[0],
        out_cotangent,
        lift_weight[0],
        proj_weight[0],
        lift_mask[0],
        proj_mask[0],
        channel_perm,
    )
    n, tok, _ = condc.shape
    tokens = n * tok
    w = gin.shape[1]
    lift_grad = tn(condc.reshape(tokens, -1), gp.reshape(tokens, w))
    proj_grad = tn(stc.reshape(tokens, -1), hid.reshape(tokens, w))
    lift_rows = lift_moment.shape[1] // BLK
    proj_rows = proj_moment.shape[1] // BLK
    lift_own = expand_blocks(lax.dynamic_slice_in_dim(lift_mask[0], dp_index * lift_rows, lift_rows, 0))
    proj_own = expand_blocks(lax.dynamic_slice_in_dim(proj_mask[0], dp_index * proj_rows, proj_rows, 0))
    lift_grad = jnp.where(lift_own, lift_grad, 0.0)
    proj_grad = jnp.where(proj_own, proj_grad, 0.0)
    local_sq = jnp.sum(lift_grad * lift_grad) + jnp.sum(proj_grad * proj_grad)
    lane = lax.broadcasted_iota(jnp.int32, (8, BLK), 1)
    row = lax.broadcasted_iota(jnp.int32, (8, BLK), 0)
    first = row == 0
    packed = jnp.where(first & (lane == 0), local_sq, 0.0) + jnp.where(
        first & (lane == 1 + core), jnp.sum(logp), 0.0
    )
    sums = sum_all(packed)
    factor = jnp.minimum(1.0, CLIP / (jnp.sqrt(sums[0, 0]) + 1e-06))
    log_total = jnp.where(core == 0, sums[0, 1], sums[0, 2])
    lift_out = adam_step(lift_grad, lift_own, lift_moment[0], lift_square[0], factor)
    proj_out = adam_step(proj_grad, proj_own, proj_moment[0], proj_square[0], factor)
    log_det = (log_total / (tokens * lift_weight.shape[1])).reshape(1)
    return (gin[None], log_det) + lift_out + proj_out


def solution(mesh):
    finer = Mesh(
        mesh.devices.reshape(NR, NR, mesh.shape["tensor"], mesh.shape["layers"]),
        ("dp_0", "dp_1", "tensor", "layers"),
    )
    tiled = P("layers", DP, "tensor")
    weight = P("layers", None, "tensor")
    return jax.shard_map(
        per_device,
        mesh=finer,
        in_specs=(tiled, P(DP, "tensor")) + (weight,) * 4 + (P("layers", None),) + (tiled,) * 4,
        out_specs=(tiled, P("layers")) + (tiled,) * 6,
        check_vma=False,
    )
```

```python
import functools

import jax
import jax.numpy as jnp
from jax import lax
from jax.experimental import pallas as pl
from jax.experimental.pallas import tpu as pltpu
from jax.sharding import Mesh
from jax.sharding import PartitionSpec as P

BLK = 128
ADAM_STEP = 10
CLIP = 4096
DP = ("dp_0", "dp_1")
MESH = pl.DeviceIdType.MESH
F32 = jnp.float32
BF16 = jnp.bfloat16

NZ = 8
NR = 4
NQ = 4

beta_one = 0.9
beta_two = 0.99
adam_eps = 1e-08


def nn(a, b):
    return jnp.dot(a, b, preferred_element_type=F32)


def nt(a, b):
    return lax.dot_general(a, b, (((1,), (1,)), ((), ())), preferred_element_type=F32)


def tn(a, b):
    return lax.dot_general(a, b, (((0,), (0,)), ((), ())), preferred_element_type=F32)


def al(i, m):
    return pl.multiple_of(i, m)


def remote(src, dst, ssem, rsem, **where):
    return pltpu.make_async_remote_copy(
        src_ref=src, dst_ref=dst, send_sem=ssem, recv_sem=rsem, device_id=where, device_id_type=MESH
    )


def far(d, h):
    return (h < NQ // 2) == (d == 0)


def both_ways(d, s, h):
    return s < 3 or far(d, h)


FIRST = [sorted(range(NQ), key=lambda h: not far(d, h)) for d in (0, 1)]
LAST = [sorted(range(NQ), key=lambda h: far(d, h)) for d in (0, 1)]


def token_kernel(
    x_ref,
    cot_ref,
    lift_hbm,
    proj_hbm,
    lmask_ref,
    pmask_ref,
    perm_ref,
    gin_out,
    stat_ref,
    lgrad_out,
    pgrad_out,
    xbuf,
    pc,
    m,
    lift,
    proj,
    cond,
    sm,
    slope,
    pre,
    stbuf,
    sbuf,
    rbuf,
    cbuf,
    c0buf,
    gbuf,
    cown,
    condc_ref,
    stc_ref,
    hid_ref,
    gp_ref,
    vec,
    zbuf,
    mid,
    pbuf,
    other,
    gin_ref,
    lgrad_ref,
    pgrad_ref,
    w_s,
    o_s,
    ag_s,
    ag_r,
    rs_s,
    rs_r,
    cs,
    cr,
    gs,
    gr,
    hs,
    hr,
    a_s,
    a_r,
    ts,
    tr,
    xs,
    xr,
    zs,
    zrv,
    ps,
    prv,
    ls,
    lr,
):
    z = lax.axis_index("tensor")
    y = lax.axis_index("dp_0")
    x = lax.axis_index("dp_1")
    core = lax.axis_index("layers")
    me = y * NR + x
    tok = x_ref.shape[0]
    half = tok // 2
    quart = tok // 4
    w = x_ref.shape[1]
    q = w // 2
    hw = NZ * q

    nq = tok // NQ

    def rows(h):
        return pl.ds(h * nq, nq)

    def zr(i):
        return lax.rem(z + NZ + i, NZ)

    zside = (zr(1), zr(-1))
    load_lift = pltpu.make_async_copy(lift_hbm, lift, w_s.at[0])
    load_proj = pltpu.make_async_copy(proj_hbm, proj, w_s.at[1])
    load_lift.start()
    load_proj.start()

    bar = pltpu.get_barrier_semaphore()
    for i in range(1, NZ):
        pl.semaphore_signal(bar, inc=1, device_id={"tensor": zr(i)}, device_id_type=MESH)
    for oy in range(NR):
        for ox in range(NR):
            if oy or ox:
                pl.semaphore_signal(
                    bar,
                    inc=1,
                    device_id={"dp_0": lax.rem(y + oy, NR), "dp_1": lax.rem(x + ox, NR)},
                    device_id_type=MESH,
                )
    pl.semaphore_signal(bar, inc=1, device_id={"layers": 1 - core}, device_id_type=MESH)

    def ag_copy(p, buf, own, s, d, h):
        origin = zr(-s) if d == 0 else zr(s)
        src = own.at[rows(h)] if s == 0 else buf.at[origin, rows(h)]
        return remote(src, buf.at[origin, rows(h)], ag_s.at[d, s, h], ag_r.at[d, s, h], tensor=zside[d])

    def ag_wait(p, buf, s, d, h):
        origin = zr(-1 - s) if d == 0 else zr(1 + s)
        ref = buf.at[origin, rows(h)]
        remote(ref, ref, ag_s.at[d, s, h], ag_r.at[d, s, h], tensor=zside[d]).wait_recv()

    def ag_start(p, buf, own):
        for k in range(NQ):
            for d in (0, 1):
                ag_copy(p, buf, own, 0, d, FIRST[d][k]).start()

    def ag_step(p, buf, own, s):
        for k in range(NQ):
            for d in (0, 1):
                h = FIRST[d][k]
                if both_ways(d, s, h):
                    ag_wait(p, buf, s, d, h)
                    if s < 3 and both_ways(d, s + 1, h):
                        ag_copy(p, buf, own, s + 1, d, h).start()
        return [zr(-1 - s), zr(1 + s)] if s < 3 else [zr(4)]

    def ag_finish(p, buf, own):
        for d in (0, 1):
            for s in range(4):
                for h in range(NQ):
                    if both_ways(d, s, h):
                        ag_copy(p, buf, own, s, d, h).wait_send()

    def rs_copy(p, s, d, h):
        return remote(
            sbuf.at[p, d, s, rows(h)],
            rbuf.at[p, d, s, rows(h)],
            rs_s.at[d, s, h],
            rs_r.at[d, s, h],
            tensor=zside[d],
        )

    def rs(p, part, tick):
        most = part(zr(4))
        for k in range(NQ // 2):
            for d in (0, 1):
                h = FIRST[d][k]
                sbuf[p, d, 0, rows(h)] = most[h * nq : (h + 1) * nq].astype(BF16)
                rs_copy(p, 0, d, h).start()
        for s in (1, 2, 3):
            mine = [part(zr(4 - s)), part(zr(s - 4))]

            def send(d, h, own):
                sbuf[p, d, s, rows(h)] = own.astype(BF16)
                rs_copy(p, s, d, h).start()

            if s == 1:
                for k in range(NQ // 2):
                    for d in (0, 1):
                        h = LAST[d][k]
                        send(d, h, mine[d][h * nq : (h + 1) * nq])
            with jax.named_scope(f"tick{s}"):
                tick(s)
            with jax.named_scope(f"w{s}"):
                for k in range(NQ // 2 if s == 1 else 0, NQ):
                    for d in (0, 1):
                        h = LAST[d][k]
                        rs_copy(p, s - 1, d, h).wait_recv()
                        own = mine[d][h * nq : (h + 1) * nq]
                        send(d, h, own + rbuf[p, d, s - 1, rows(h)].astype(F32))

        def end():
            own = part(z)
            with jax.named_scope("w4"):
                for d in (0, 1):
                    for h in range(NQ):
                        rs_copy(p, 3, d, h).wait_recv()
            return own + rbuf[p, 0, 3].astype(F32) + rbuf[p, 1, 3].astype(F32)

        return end

    def rs_finish(p):
        for d in (0, 1):
            for s in range(4):
                for h in range(NQ):
                    if s > 0 or far(d, h):
                        rs_copy(p, s, d, h).wait_send()

    def along(axis, i):
        if axis == "dp_1":
            return {"dp_1": lax.rem(x + NR + i, NR)}
        return {"dp_0": lax.rem(y + NR + i, NR)}

    def slot(buf, stage, h, off, r):
        axis = ("dp_1", "dp_0")[(h + stage) % 2]
        yy, xx = (y, lax.rem(x + NR + off, NR)) if axis == "dp_1" else (lax.rem(y + NR + off, NR), x)
        if stage == 0:
            return buf.at[yy, xx, r]
        return buf.at[yy, :, r] if axis == "dp_0" else buf.at[:, xx, r]

    def xy_rows(h, t, d):
        if t == 0:
            return pl.ds(h * half, half)
        return pl.ds(h * half + d * quart, quart)

    def xy_copy(p, buf, stage, h, t, d):
        axis = ("dp_1", "dp_0")[(h + stage) % 2]
        step = 1 if d == 0 else -1
        src = slot(buf, stage, h, 0 if t == 0 else -step, xy_rows(h, t, d))
        return remote(
            src, src, xs.at[p, stage, h, t, d], xr.at[p, stage, h, t, d], **along(axis, step)
        )

    def xy_wait(p, buf, stage, h, t, d):
        axis = ("dp_1", "dp_0")[(h + stage) % 2]
        step = 1 if d == 0 else -1
        ref = slot(buf, stage, h, -step if t == 0 else -2 * step, xy_rows(h, t, d))
        remote(
            ref, ref, xs.at[p, stage, h, t, d], xr.at[p, stage, h, t, d], **along(axis, step)
        ).wait_recv()

    def xy_tick(p, buf, k):
        stage, t = k // 2, k % 2
        with jax.named_scope(f"xy{p}{k}"):
            if k:
                ps_, pt = (k - 1) // 2, (k - 1) % 2
                for h in (0, 1):
                    for d in (0, 1):
                        xy_wait(p, buf, ps_, h, pt, d)
            if k < 4:
                for h in (0, 1):
                    for d in (0, 1):
                        xy_copy(p, buf, stage, h, t, d).start()

    def xy_finish(p, buf):
        for stage in (0, 1):
            for h in (0, 1):
                for t in (0, 1):
                    for d in (0, 1):
                        xy_copy(p, buf, stage, h, t, d).wait_send()

    def mask_lift(i, _):
        r = pl.ds(al(i * BLK, BLK), BLK)
        for c in range(w // BLK):
            cc = pl.ds(c * BLK, BLK)
            keep = lmask_ref[c, i].astype(F32)
            lift[r, cc] = (lift[r, cc].astype(F32) * keep).astype(BF16)
        return 0

    def mask_proj(i, _):
        r = pl.ds(al(i * BLK, BLK), BLK)
        for c in range(w // BLK):
            cc = pl.ds(c * BLK, BLK)
            keep = pmask_ref[c, i].astype(F32)
            proj[r, cc] = (proj[r, cc].astype(F32) * keep).astype(BF16)
        return 0

    ca_perm = pl.ds(al(z * q, q), q)
    mv_perm = pl.ds(al(hw + z * q, q), q)

    def hot(base, order):
        at = lax.broadcasted_iota(jnp.int32, (BLK, q), 0) + base
        return jnp.where(at == order, 1.0, 0.0).astype(BF16)

    def build(i, _):
        base = i * BLK
        r = pl.ds(al(base, BLK), BLK)
        for c in range(hw // q):
            cc = pl.ds(c * q, q)
            pc[r, cc] = hot(base, perm_ref[:, cc])
        m[r, pl.ds(w, q)] = hot(base, perm_ref[:, ca_perm])
        m[r, pl.ds(w + q, q)] = hot(base, perm_ref[:, mv_perm])
        return 0

    def of(origin):
        return pl.ds(al(origin * w, w), w)

    def spread(origin):
        with jax.named_scope("spread"):
            m[of(origin), pl.ds(0, w)] = nn(pc[of(origin), :], lift[...]).astype(BF16)

    def times(origin):
        return nn(xbuf[origin], m[of(origin), pl.ds(0, w)])

    def pick(c, _):
        cc = pl.ds(al(c * q, q), q)
        got = nn(xbuf[0], pc[pl.ds(0, w), cc])
        for o in range(1, NZ):
            got = got + nn(xbuf[o], pc[pl.ds(o * w, w), cc])
        cond[:, cc] = got.astype(BF16)
        return 0

    with jax.named_scope("build"):
        lax.fori_loop(0, 2 * hw // BLK, build, 0)
    xbuf[z] = x_ref[...]
    load_lift.wait()
    lax.fori_loop(0, hw // BLK, mask_lift, 0)
    spread(z)
    spread(zr(-1))
    with jax.named_scope("barrier"):
        pl.semaphore_wait(bar, NZ - 1 + NR * NR - 1 + 1)
    ag_start(0, xbuf, x_ref)

    @pl.when(core == 1)
    def _():
        for e in (0, 1):
            dest = lax.rem(2 * z + e, NZ)
            piece = cot_ref.at[:, pl.ds(e * q, q)]
            land = cbuf.at[:, pl.ds(al((z // 4) * q, q), q)]

            @pl.when(dest != z)
            def _():
                remote(piece, land, cs.at[e], cr.at[z // 4], tensor=dest).start()

            @pl.when(dest == z)
            def _():
                cbuf[:, pl.ds(al((z // 4) * q, q), q)] = cot_ref[:, pl.ds(e * q, q)]

    spread(zr(1))
    pre[...] = times(z)
    spread(zr(-2))
    spread(zr(2))
    load_proj.wait()
    with jax.named_scope("mask_proj"):
        lax.fori_loop(0, 2 * hw // BLK, mask_proj, 0)
    for s in range(4):
        with jax.named_scope(f"agx{s}"):
            came = ag_step(0, xbuf, x_ref, s)
        if s < 3:
            spread((zr(-3), zr(3), zr(4))[s])
        for origin in came:
            pre[...] += times(origin)

    ag_finish(0, xbuf, x_ref)

    squash = jax.nn.sigmoid(pre[...])
    slope[...] = squash * (1.0 + pre[...] * (1.0 - squash))
    hid_ref[y, x] = (pre[...] * squash).astype(BF16)
    xy_tick(0, hid_ref, 0)

    hidden = hid_ref[y, x]

    def proj_rows(d, k):
        return pl.ds(al(k * hw + d * q, q), q)

    def shared_part(d):
        return jnp.concatenate(
            [nt(hidden, proj[proj_rows(d, 0), :]), nt(hidden, proj[proj_rows(d, 1), :])], axis=1
        )

    def shared_tick(s):
        if s == 1:
            got = nn(xbuf[0], m[pl.ds(0, w), pl.ds(w + q, q)])
            for o in range(1, NZ):
                got = got + nn(xbuf[o], m[pl.ds(o * w, w), pl.ds(w + q, q)])
            sm[:, pl.ds(q, q)] = got

    with jax.named_scope("rs_shared"):
        shared = rs(0, shared_part, shared_tick)()
    rs_finish(0)
    raw = shared[:, :q] + 2.0
    scale = jax.nn.sigmoid(raw)
    sm[:, pl.ds(0, q)] = scale
    sm[:, pl.ds(q, q)] += shared[:, q:]
    logs = jnp.minimum(raw, 0.0) - jnp.log1p(jnp.exp(-jnp.abs(raw)))
    logs = jnp.sum(logs.reshape(tok // 8, 8, q), axis=0)
    vec[1] = logs[:, :BLK] + logs[:, BLK:]
    xy_tick(0, hid_ref, 1)

    def cond_copy(o):
        oy, ox = o // NR, o % NR
        ty, tx = lax.rem(y + oy, NR), lax.rem(x + ox, NR)
        return remote(
            cond.at[:, pl.ds(al((ty * NR + tx) * BLK, BLK), BLK)],
            condc_ref.at[me],
            a_s,
            a_r,
            dp_0=ty,
            dp_1=tx,
        )

    def all_of(buf, ssem, rsem):
        ref = buf.at[pl.ds(0, buf.shape[0] - 1)]
        return remote(ref, ref, ssem, rsem, dp_0=lax.rem(y + 1, NR))

    def permute_tokens(lo, hi):
        with jax.named_scope("permute"):
            lax.fori_loop(lo, hi, pick, 0)
        if hi == hw // q:
            for o in range(1, NR * NR):
                cond_copy(o).start()
            condc_ref[me] = cond[:, pl.ds(al(me * BLK, BLK), BLK)]

    @pl.when(core == 1)
    def _():
        for k in (0, 1):

            @pl.when(4 * k + z // 2 != z)
            def _():
                ref = cbuf.at[:, pl.ds(k * q, q)]
                remote(ref, ref, cs.at[0], cr.at[k], tensor=z).wait_recv()

        cown[...] = cbuf[...]

    @pl.when(core == 0)
    def _():
        permute_tokens(0, hw // q)
        xy_tick(0, hid_ref, 2)
        with jax.named_scope("handwait"):
            remote(gbuf, c0buf, hs, hr, layers=1 - core).wait_recv()
        cown[...] = c0buf[...]

    ca = cown[:, pl.ds(0, q)]
    cb = cown[:, pl.ds(q, q)].astype(F32)
    scale = sm[:, pl.ds(0, q)]
    keep_part = 1.0 - scale
    shift_grad = (cb * scale).astype(BF16)
    raw_grad = (cb * sm[:, pl.ds(q, q)] * scale * keep_part - keep_part).astype(BF16)
    stbuf[z, :, pl.ds(0, q)] = raw_grad
    stbuf[z, :, pl.ds(q, q)] = shift_grad
    own_st = stbuf.at[z]
    ag_start(1, stbuf, own_st)

    def st_copy(origin, k):
        to = origin + NZ * k
        return remote(
            stbuf.at[origin, :, pl.ds(k * q, q)],
            stc_ref.at[me],
            ts,
            tr,
            dp_0=to // NR,
            dp_1=lax.rem(to, NR),
        )

    def st_send(origin):
        for k in (0, 1):

            @pl.when(origin + NZ * k != me)
            def _():
                st_copy(origin, k).start()

            @pl.when(origin + NZ * k == me)
            def _():
                stc_ref[me] = stbuf[origin, :, pl.ds(k * q, q)]

    def act(origin):
        return nn(stbuf[origin, :, pl.ds(0, q)], proj[proj_rows(origin, 0), :]) + nn(
            stbuf[origin, :, pl.ds(q, q)], proj[proj_rows(origin, 1), :]
        )

    pre[...] = act(z)
    st_send(z)

    @pl.when(core == 1)
    def _():
        permute_tokens(0, 5)

    for s in range(4):
        with jax.named_scope(f"agst{s}"):
            came = ag_step(1, stbuf, own_st, s)
        if s < 2:
            for origin in came:
                st_send(origin)
        for origin in came:
            pre[...] += act(origin)
        if s == 0:

            @pl.when(core == 1)
            def _():
                permute_tokens(5, hw // q)

        if s == 1:

            @pl.when(core == 0)
            def _():
                xy_tick(0, hid_ref, 3)

        if s == 2:

            @pl.when(core == 1)
            def _():
                xy_tick(0, hid_ref, 2)

    grad_pre = (pre[...] * slope[...]).astype(BF16)
    gp_ref[y, x] = grad_pre
    xy_tick(1, gp_ref, 0)

    lhs = jnp.concatenate([grad_pre, ca, shift_grad], axis=1)

    def in_rows(d, k):
        there = jnp.where(core == 1, k * hw + d * q, (2 * d + k) * q)
        return pl.ds(al(there, q), q)

    def in_part(d):
        return jnp.concatenate([nt(lhs, m[in_rows(d, 0), :]), nt(lhs, m[in_rows(d, 1), :])], axis=1)

    def in_tick(s):
        @pl.when(core == 0)
        def _():
            xy_tick(1, gp_ref, s)

        if s == 1:
            for i in (-3, 3, 4):
                st_send(zr(i))

    with jax.named_scope("rs_in"):
        end = rs(1, in_part, in_tick)

    def gsend(k):
        return remote(
            cown.at[:, pl.ds(k * q, q)],
            gbuf.at[:, pl.ds(al(lax.rem(z, 2) * q, q), q)],
            gs.at[k],
            gr.at[lax.rem(z, 2)],
            tensor=4 * k + z // 2,
        )

    @pl.when(core == 1)
    def _():
        cown[...] = end().astype(BF16)
        remote(cown, c0buf, hs, hr, layers=1 - core).start()
        for k in (0, 1):

            @pl.when(4 * k + z // 2 != z)
            def _():
                gsend(k).start()

            @pl.when(4 * k + z // 2 == z)
            def _():
                gbuf[:, pl.ds(al(lax.rem(z, 2) * q, q), q)] = cown[:, pl.ds(k * q, q)]

        xy_tick(1, gp_ref, 1)
        xy_tick(0, hid_ref, 3)
        xy_tick(1, gp_ref, 2)
        xy_tick(0, hid_ref, 4)
        xy_tick(1, gp_ref, 3)

    tokens = NR * NR * tok

    def squares(g):
        g = jnp.sum((g * g).reshape(g.shape[0] // 8, 8, w), axis=0)
        out = g[:, :BLK]
        for c in range(1, w // BLK):
            out = out + g[:, c * BLK : (c + 1) * BLK]
        return out

    @pl.when(core == 0)
    def _():
        xy_tick(0, hid_ref, 4)

    with jax.named_scope("stcome"):
        all_of(stc_ref, ts, tr).wait_recv()
    with jax.named_scope("pgrad"):
        pgrad_ref[...] = tn(stc_ref[...].reshape(tokens, q), hid_ref[...].reshape(tokens, w))
    for b in range(q // BLK):
        for c in range(w // BLK):
            keep = pmask_ref[c, me * (q // BLK) + b].astype(F32)
            pgrad_ref[pl.ds(b * BLK, BLK), pl.ds(c * BLK, BLK)] *= keep
    vec[0] = squares(pgrad_ref[...])
    with jax.named_scope("condwait"):
        all_of(condc_ref, a_s, a_r).wait_recv()
    xy_tick(1, gp_ref, 4)
    with jax.named_scope("lgrad"):
        lgrad_ref[...] = tn(condc_ref[...].reshape(tokens, BLK), gp_ref[...].reshape(tokens, w))
    for c in range(w // BLK):
        keep = lmask_ref[c, me].astype(F32)
        lgrad_ref[:, pl.ds(c * BLK, BLK)] *= keep
    vec[0] += squares(lgrad_ref[...])

    save_pgrad = pltpu.make_async_copy(pgrad_ref, pgrad_out, o_s.at[0])
    save_lgrad = pltpu.make_async_copy(lgrad_ref, lgrad_out, o_s.at[1])
    save_gin = pltpu.make_async_copy(gin_ref, gin_out, o_s.at[2])
    def zcopy(i):
        return remote(vec, zbuf.at[z], zs, zrv, tensor=zr(i))

    for i in range(1, NZ):
        zcopy(i).start()
    zbuf[z] = vec[...]
    save_pgrad.start()
    save_lgrad.start()

    @pl.when(core == 1)
    def _():
        for e in (0, 1):

            @pl.when(lax.rem(2 * z + e, NZ) != z)
            def _():
                ref = gbuf.at[:, pl.ds(e * q, q)]
                remote(ref, ref, gs.at[0], gr.at[e], tensor=z).wait_recv()

        gin_ref[...] = gbuf[...].astype(F32)

    @pl.when(core == 0)
    def _():
        gin_ref[...] = end()

    save_gin.start()
    with jax.named_scope("zsum"):
        all_of(zbuf, zs, zrv).wait_recv()
    mid[...] = jnp.sum(zbuf[...], axis=0)

    def pcopy(o):
        ty, tx = lax.rem(y + o // NR, NR), lax.rem(x + o % NR, NR)
        return remote(mid, pbuf.at[me], ps, prv, dp_0=ty, dp_1=tx)

    for o in range(1, NR * NR):
        pcopy(o).start()
    pbuf[me] = mid[...]
    with jax.named_scope("psum"):
        all_of(pbuf, ps, prv).wait_recv()
    other[0] = jnp.sum(pbuf[...], axis=0)
    swap = remote(other.at[0], other.at[1], ls, lr, layers=1 - core)
    swap.start()

    @pl.when(core == 1)
    def _():
        remote(cown, c0buf, hs, hr, layers=1 - core).wait_send()
        for k in (0, 1):

            @pl.when(4 * k + z // 2 != z)
            def _():
                gsend(k).wait_send()

        for e in (0, 1):
            dest = lax.rem(2 * z + e, NZ)

            @pl.when(dest != z)
            def _():
                ref = cot_ref.at[:, pl.ds(e * q, q)]
                remote(ref, ref, cs.at[e], cr.at[0], tensor=dest).wait_send()

    all_of(condc_ref, a_s, a_r).wait_send()
    all_of(stc_ref, ts, tr).wait_send()
    ag_finish(1, stbuf, own_st)
    rs_finish(1)
    xy_finish(0, hid_ref)
    xy_finish(1, gp_ref)
    all_of(zbuf, zs, zrv).wait_send()
    all_of(pbuf, ps, prv).wait_send()
    save_pgrad.wait()
    save_lgrad.wait()
    save_gin.wait()
    with jax.named_scope("swap"):
        swap.wait_recv()
    stat_ref[0] = other[0, 0] + other[1, 0]
    stat_ref[1] = other[0, 1]
    swap.wait_send()


def token_side(x, cot, lift_w, proj_w, lmask, pmask, perm):
    tok, w = x.shape
    hw = lift_w.shape[0]
    feat = 2 * hw
    q = w // 2
    dma = pltpu.SemaphoreType.DMA
    vm = pl.BlockSpec(memory_space=pltpu.VMEM)
    sm = pl.BlockSpec(memory_space=pltpu.SMEM)
    hbm = pl.BlockSpec(memory_space=pl.ANY)
    n = NR * NR
    return pl.pallas_call(
        token_kernel,
        out_shape=(
            jax.ShapeDtypeStruct((tok, w), F32),
            jax.ShapeDtypeStruct((2, 8, BLK), F32),
            jax.ShapeDtypeStruct((BLK, w), F32),
            jax.ShapeDtypeStruct((q, w), F32),
        ),
        in_specs=[vm, vm, hbm, hbm, sm, sm, vm],
        out_specs=(hbm, vm, hbm, hbm),
        scratch_shapes=[
            pltpu.VMEM((NZ, tok, w), BF16),
            pltpu.VMEM((feat, hw), BF16),
            pltpu.VMEM((feat, 2 * w), BF16),
            pltpu.VMEM((hw, w), BF16),
            pltpu.VMEM((feat, w), BF16),
            pltpu.VMEM((tok, hw), BF16),
            pltpu.VMEM((tok, w), F32),
            pltpu.VMEM((tok, w), F32),
            pltpu.VMEM((tok, w), F32),
            pltpu.VMEM((NZ, tok, w), BF16),
            pltpu.VMEM((2, 2, 4, tok, w), BF16),
            pltpu.VMEM((2, 2, 4, tok, w), BF16),
            pltpu.VMEM((tok, w), BF16),
            pltpu.VMEM((tok, w), BF16),
            pltpu.VMEM((tok, w), BF16),
            pltpu.VMEM((tok, w), BF16),
            pltpu.VMEM((n, tok, BLK), BF16),
            pltpu.VMEM((n, tok, q), BF16),
            pltpu.VMEM((NR, NR, tok, w), BF16),
            pltpu.VMEM((NR, NR, tok, w), BF16),
            pltpu.VMEM((2, 8, BLK), F32),
            pltpu.VMEM((NZ, 2, 8, BLK), F32),
            pltpu.VMEM((2, 8, BLK), F32),
            pltpu.VMEM((n, 2, 8, BLK), F32),
            pltpu.VMEM((2, 2, 8, BLK), F32),
            pltpu.VMEM((tok, w), F32),
            pltpu.VMEM((BLK, w), F32),
            pltpu.VMEM((q, w), F32),
            dma((2,)),
            dma((3,)),
            dma((2, 4, NQ)),
            dma((2, 4, NQ)),
            dma((2, 4, NQ)),
            dma((2, 4, NQ)),
            dma((2,)),
            dma((2,)),
            dma((2,)),
            dma((2,)),
            dma,
            dma,
            dma,
            dma,
            dma,
            dma,
            dma((2, 2, 2, 2, 2)),
            dma((2, 2, 2, 2, 2)),
            dma,
            dma,
            dma,
            dma,
            dma,
            dma,
        ],
        compiler_params=pltpu.CompilerParams(
            collective_id=0, has_side_effects=True, vmem_limit_bytes=64 * 1024 * 1024 - 64 * 1024
        ),
        name="token_side",
    )(x, cot, lift_w, proj_w, lmask, pmask, perm)


def adam_kernel(
    lmask_ref,
    pmask_ref,
    stat_ref,
    lgrad_hbm,
    lmom_hbm,
    lsq_hbm,
    pgrad_hbm,
    pmom_hbm,
    psq_hbm,
    gin_hbm,
    lfirst_out,
    lsecond_out,
    lupdate_out,
    pfirst_out,
    psecond_out,
    pupdate_out,
    gin_out,
    log_ref,
    gin,
    grads,
    moms,
    sqs,
    news,
    in_s,
    out_s,
    gin_s,
    *,
    entries,
):
    me = lax.axis_index("dp_0") * NR + lax.axis_index("dp_1")
    n, rows, w = grads.shape
    blocks = []
    for b in range(n):
        r = pl.ds((b - 1) * rows, rows)
        if b == 0:
            ins = [lgrad_hbm, lmom_hbm.at[0], lsq_hbm.at[0]]
            outs = [lfirst_out.at[0], lsecond_out.at[0], lupdate_out.at[0]]
        else:
            ins = [pgrad_hbm.at[r], pmom_hbm.at[0, r], psq_hbm.at[0, r]]
            outs = [pfirst_out.at[0, r], psecond_out.at[0, r], pupdate_out.at[0, r]]
        loads = [
            pltpu.make_async_copy(ref, buf.at[b], in_s.at[b, k])
            for k, (ref, buf) in enumerate(zip(ins, (grads, moms, sqs)))
        ]
        saves = [pltpu.make_async_copy(news.at[b, k], ref, out_s.at[b, k]) for k, ref in enumerate(outs)]
        blocks.append((loads, saves))
    for loads, _ in blocks:
        for c in loads:
            c.start()
    gin_load = pltpu.make_async_copy(gin_hbm, gin, gin_s.at[0])
    gin_save = pltpu.make_async_copy(gin, gin_out.at[0], gin_s.at[1])
    gin_load.start()
    total = jnp.sum(stat_ref[0], keepdims=True)
    factor = jnp.minimum(1.0, CLIP / (jnp.sqrt(total) + 1e-06))
    log_ref[0] = jnp.sum(stat_ref[1]) * (1.0 / entries)
    bias_one = 1.0 - beta_one**ADAM_STEP
    bias_two = 1.0 - beta_two**ADAM_STEP
    for b, (loads, saves) in enumerate(blocks):
        for c in loads:
            c.wait()
        for c in range(w // BLK):
            cc = pl.ds(c * BLK, BLK)
            keep = (lmask_ref[c, me] if b == 0 else pmask_ref[c, me * (n - 1) + b - 1]) > 0
            moment = moms[b, :, cc]
            square = sqs[b, :, cc]
            scaled = grads[b, :, cc] * factor
            first = jnp.where(keep, beta_one * moment + (1.0 - beta_one) * scaled, moment)
            second = jnp.where(keep, beta_two * square + (1.0 - beta_two) * scaled * scaled, square)
            update = (first * (1.0 / bias_one)) / (jnp.sqrt(second * (1.0 / bias_two)) + adam_eps)
            news[b, 0, :, cc] = first
            news[b, 1, :, cc] = second
            news[b, 2, :, cc] = jnp.where(keep, update, 0.0)
        for c in saves:
            c.start()
    gin_load.wait()
    gin_save.start()
    gin_save.wait()
    for _, saves in blocks:
        for c in saves:
            c.wait()


def adam(entries, lmask, pmask, stat, lgrad, lmom, lsq, pgrad, pmom, psq, gin):
    dma = pltpu.SemaphoreType.DMA
    vm = pl.BlockSpec(memory_space=pltpu.VMEM)
    smem = pl.BlockSpec(memory_space=pltpu.SMEM)
    hbm = pl.BlockSpec(memory_space=pl.ANY)
    rows, w = lgrad.shape
    n = 1 + pgrad.shape[0] // rows
    like = jax.ShapeDtypeStruct
    return pl.pallas_call(
        functools.partial(adam_kernel, entries=entries),
        out_shape=(like(lmom.shape, F32),) * 3
        + (like(pmom.shape, F32),) * 3
        + (like((1,) + gin.shape, F32), like((1,), F32)),
        in_specs=[smem, smem, vm] + [hbm] * 7,
        out_specs=(hbm,) * 7 + (smem,),
        scratch_shapes=[
            pltpu.VMEM(gin.shape, F32),
            pltpu.VMEM((n, rows, w), F32),
            pltpu.VMEM((n, rows, w), F32),
            pltpu.VMEM((n, rows, w), F32),
            pltpu.VMEM((n, 3, rows, w), F32),
            dma((n, 3)),
            dma((n, 3)),
            dma((2,)),
        ],
        name="adam",
    )(lmask, pmask, stat, lgrad, lmom, lsq, pgrad, pmom, psq, gin)


def per_device(
    section_input,
    out_cotangent,
    lift_weight,
    proj_weight,
    lift_mask,
    proj_mask,
    channel_perm,
    lift_moment,
    lift_square,
    proj_moment,
    proj_square,
):
    lmask, pmask = lift_mask[0].T, proj_mask[0].T
    gin, stat, lift_grad, proj_grad = token_side(
        section_input[0], out_cotangent, lift_weight[0], proj_weight[0], lmask, pmask, channel_perm
    )
    tokens = NR * NR * gin.shape[0]
    *stepped, input_grad, log_det = adam(
        tokens * lift_weight.shape[1],
        lmask,
        pmask,
        stat,
        lift_grad,
        lift_moment,
        lift_square,
        proj_grad,
        proj_moment,
        proj_square,
        gin,
    )
    return (input_grad, log_det) + tuple(stepped)


def solution(mesh):
    finer = Mesh(
        mesh.devices.reshape(NR, NR, mesh.shape["tensor"], mesh.shape["layers"]),
        ("dp_0", "dp_1", "tensor", "layers"),
    )
    tiled = P("layers", DP, "tensor")
    weight = P("layers", None, "tensor")
    return jax.shard_map(
        per_device,
        mesh=finer,
        in_specs=(tiled, P(DP, "tensor")) + (weight,) * 4 + (P("layers", None),) + (tiled,) * 4,
        out_specs=(tiled, P("layers")) + (tiled,) * 6,
        check_vma=False,
    )
```

```python
import functools

import jax
import jax.numpy as jnp
from jax import lax
from jax.experimental import pallas as pl
from jax.experimental.pallas import tpu as pltpu
from jax.sharding import Mesh
from jax.sharding import PartitionSpec as P

BLK = 128
ADAM_STEP = 10
CLIP = 4096
DP = ("dp_0", "dp_1")
MESH = pl.DeviceIdType.MESH
F32 = jnp.float32
BF16 = jnp.bfloat16

NZ = 8
NR = 4
NQ = 4

beta_one = 0.9
beta_two = 0.99
adam_eps = 1e-08


def nn(a, b):
    return jnp.dot(a, b, preferred_element_type=F32)


def nt(a, b):
    return lax.dot_general(a, b, (((1,), (1,)), ((), ())), preferred_element_type=F32)


def tn(a, b):
    return lax.dot_general(a, b, (((0,), (0,)), ((), ())), preferred_element_type=F32)


def al(i, m):
    return pl.multiple_of(i, m)


def remote(src, dst, ssem, rsem, **where):
    return pltpu.make_async_remote_copy(
        src_ref=src, dst_ref=dst, send_sem=ssem, recv_sem=rsem, device_id=where, device_id_type=MESH
    )


def far(d, h):
    return (h < NQ // 2) == (d == 0)


def both_ways(d, s, h):
    return s < 3 or far(d, h)


FIRST = [sorted(range(NQ), key=lambda h: not far(d, h)) for d in (0, 1)]
LAST = [sorted(range(NQ), key=lambda h: far(d, h)) for d in (0, 1)]


def token_kernel(
    x_ref,
    cot_ref,
    lift_hbm,
    proj_hbm,
    lmask_ref,
    pmask_ref,
    perm_ref,
    gin_out,
    stat_ref,
    lgrad_out,
    pgrad_out,
    xbuf,
    pc,
    m,
    lift,
    proj,
    cond,
    sm,
    slope,
    pre,
    stbuf,
    sbuf,
    rbuf,
    cbuf,
    c0buf,
    gbuf,
    cown,
    condc_ref,
    stc_ref,
    hid_ref,
    gp_ref,
    vec,
    zbuf,
    mid,
    pbuf,
    other,
    gin_ref,
    lgrad_ref,
    pgrad_ref,
    w_s,
    o_s,
    ag_s,
    ag_r,
    rs_s,
    rs_r,
    cs,
    cr,
    gs,
    gr,
    hs,
    hr,
    a_s,
    a_r,
    ts,
    tr,
    xs,
    xr,
    zs,
    zrv,
    ps,
    prv,
    ls,
    lr,
):
    z = lax.axis_index("tensor")
    y = lax.axis_index("dp_0")
    x = lax.axis_index("dp_1")
    core = lax.axis_index("layers")
    me = y * NR + x
    tok = x_ref.shape[0]
    half = tok // 2
    quart = tok // 4
    w = x_ref.shape[1]
    q = w // 2
    hw = NZ * q

    nq = tok // NQ

    def rows(h):
        return pl.ds(h * nq, nq)

    def zr(i):
        return lax.rem(z + NZ + i, NZ)

    zside = (zr(1), zr(-1))
    load_lift = pltpu.make_async_copy(lift_hbm, lift, w_s.at[0])
    load_proj = pltpu.make_async_copy(proj_hbm, proj, w_s.at[1])
    load_lift.start()
    load_proj.start()

    bar = pltpu.get_barrier_semaphore()
    for i in range(1, NZ):
        pl.semaphore_signal(bar, inc=1, device_id={"tensor": zr(i)}, device_id_type=MESH)
    for oy in range(NR):
        for ox in range(NR):
            if oy or ox:
                pl.semaphore_signal(
                    bar,
                    inc=1,
                    device_id={"dp_0": lax.rem(y + oy, NR), "dp_1": lax.rem(x + ox, NR)},
                    device_id_type=MESH,
                )
    pl.semaphore_signal(bar, inc=1, device_id={"layers": 1 - core}, device_id_type=MESH)

    def ag_copy(p, buf, own, s, d, h):
        origin = zr(-s) if d == 0 else zr(s)
        src = own.at[rows(h)] if s == 0 else buf.at[origin, rows(h)]
        return remote(src, buf.at[origin, rows(h)], ag_s, ag_r.at[d, s, h], tensor=zside[d])

    def ag_wait(p, buf, s, d, h):
        origin = zr(-1 - s) if d == 0 else zr(1 + s)
        ref = buf.at[origin, rows(h)]
        remote(ref, ref, ag_s, ag_r.at[d, s, h], tensor=zside[d]).wait_recv()

    def ag_start(p, buf, own):
        for k in range(NQ):
            for d in (0, 1):
                ag_copy(p, buf, own, 0, d, FIRST[d][k]).start()

    def ag_step(p, buf, own, s):
        for k in range(NQ):
            for d in (0, 1):
                h = FIRST[d][k]
                if both_ways(d, s, h):
                    ag_wait(p, buf, s, d, h)
                    if s < 3 and both_ways(d, s + 1, h):
                        ag_copy(p, buf, own, s + 1, d, h).start()
        return [zr(-1 - s), zr(1 + s)] if s < 3 else [zr(4)]

    def ring_sent(ssem, rsem):
        ref = xbuf.at[pl.ds(0, NZ - 1)]
        remote(ref, ref, ssem, rsem.at[0, 0, 0], tensor=zside[0]).wait_send()

    def rs_copy(p, s, d, h):
        return remote(
            sbuf.at[p, d, s, rows(h)],
            rbuf.at[p, d, s, rows(h)],
            rs_s,
            rs_r.at[d, s, h],
            tensor=zside[d],
        )

    def rs(p, part, tick):
        most = part(zr(4))
        for k in range(NQ // 2):
            for d in (0, 1):
                h = FIRST[d][k]
                sbuf[p, d, 0, rows(h)] = most[h * nq : (h + 1) * nq].astype(BF16)
                rs_copy(p, 0, d, h).start()
        for s in (1, 2, 3):
            mine = [part(zr(4 - s)), part(zr(s - 4))]

            def send(d, h, own):
                sbuf[p, d, s, rows(h)] = own.astype(BF16)
                rs_copy(p, s, d, h).start()

            if s == 1:
                for k in range(NQ // 2):
                    for d in (0, 1):
                        h = LAST[d][k]
                        send(d, h, mine[d][h * nq : (h + 1) * nq])
            with jax.named_scope(f"tick{s}"):
                tick(s)
            with jax.named_scope(f"w{s}"):
                for k in range(NQ // 2 if s == 1 else 0, NQ):
                    for d in (0, 1):
                        h = LAST[d][k]
                        rs_copy(p, s - 1, d, h).wait_recv()
                        own = mine[d][h * nq : (h + 1) * nq]
                        send(d, h, own + rbuf[p, d, s - 1, rows(h)].astype(F32))

        def end():
            own = part(z)
            with jax.named_scope("w4"):
                for d in (0, 1):
                    for h in range(NQ):
                        rs_copy(p, 3, d, h).wait_recv()
            return own + rbuf[p, 0, 3].astype(F32) + rbuf[p, 1, 3].astype(F32)

        return end

    def along(axis, i):
        if axis == "dp_1":
            return {"dp_1": lax.rem(x + NR + i, NR)}
        return {"dp_0": lax.rem(y + NR + i, NR)}

    def slot(buf, stage, h, off, r):
        axis = ("dp_1", "dp_0")[(h + stage) % 2]
        yy, xx = (y, lax.rem(x + NR + off, NR)) if axis == "dp_1" else (lax.rem(y + NR + off, NR), x)
        if stage == 0:
            return buf.at[yy, xx, r]
        return buf.at[yy, :, r] if axis == "dp_0" else buf.at[:, xx, r]

    def xy_rows(h, t, d):
        if t == 0:
            return pl.ds(h * half, half)
        return pl.ds(h * half + d * quart, quart)

    def xy_copy(p, buf, stage, h, t, d):
        axis = ("dp_1", "dp_0")[(h + stage) % 2]
        step = 1 if d == 0 else -1
        off = 0 if t == 0 else -step
        rr = xy_rows(h, t, d)
        if stage == 0 and t == 1:
            step, off, rr = 2, 0, xy_rows(h, 0, 0)
        src = slot(buf, stage, h, off, rr)
        return remote(src, src, xs.at[p], xr.at[p, stage, h, t, d], **along(axis, step))

    def xy_wait(p, buf, stage, h, t, d):
        step = 1 if d == 0 else -1
        off = -step if t == 0 else -2 * step
        rr = xy_rows(h, 0 if stage == 0 else t, d)
        ref = slot(buf, stage, h, off, rr)
        remote(ref, ref, xs.at[p], xr.at[p, stage, h, t, d], tensor=zside[0]).wait_recv()

    def xy_each(stage, t, act_on):
        for h in (0, 1):
            for d in (0,) if stage == 0 and t == 1 else (0, 1):
                act_on(stage, h, t, d)

    def xy_tick(p, buf, k):
        with jax.named_scope(f"xy{p}{k}"):
            for stage, t in ((), ((0, 0), (0, 1)), ((1, 0),), ((1, 1),))[k]:
                xy_each(stage, t, lambda *a: xy_wait(p, buf, *a))
            for stage, t in (((0, 0), (0, 1)), ((1, 0),), ((1, 1),), ())[k]:
                xy_each(stage, t, lambda *a: xy_copy(p, buf, *a).start())

    def xy_finish(p):
        ref = m.at[pl.ds(0, (NR * NR - 1) * tok // 2)]
        remote(ref, ref, xs.at[p], xr.at[p, 0, 0, 0, 0], tensor=zside[0]).wait_send()

    def mask_lift(i, _):
        r = pl.ds(al(i * BLK, BLK), BLK)
        for c in range(w // BLK):
            cc = pl.ds(c * BLK, BLK)
            keep = lmask_ref[c, i].astype(F32)
            lift[r, cc] = (lift[r, cc].astype(F32) * keep).astype(BF16)
        return 0

    def mask_proj(i, _):
        r = pl.ds(al(i * BLK, BLK), BLK)
        for c in range(w // BLK):
            cc = pl.ds(c * BLK, BLK)
            keep = pmask_ref[c, i].astype(F32)
            proj[r, cc] = (proj[r, cc].astype(F32) * keep).astype(BF16)
        return 0

    ca_perm = pl.ds(al(z * q, q), q)
    mv_perm = pl.ds(al(hw + z * q, q), q)

    def hot(base, order):
        at = lax.broadcasted_iota(jnp.int32, (BLK, q), 0) + base
        return jnp.where(at == order, 1.0, 0.0).astype(BF16)

    def build(i, _):
        base = i * BLK
        r = pl.ds(al(base, BLK), BLK)
        for c in range(hw // q):
            cc = pl.ds(c * q, q)
            pc[r, cc] = hot(base, perm_ref[:, cc])
        m[r, pl.ds(w, q)] = hot(base, perm_ref[:, ca_perm])
        m[r, pl.ds(w + q, q)] = hot(base, perm_ref[:, mv_perm])
        return 0

    def of(origin):
        return pl.ds(al(origin * w, w), w)

    def spread(origin):
        with jax.named_scope("spread"):
            m[of(origin), pl.ds(0, w)] = nn(pc[of(origin), :], lift[...]).astype(BF16)

    def times(origin):
        return nn(xbuf[origin], m[of(origin), pl.ds(0, w)])

    def pick(c, _):
        cc = pl.ds(al(c * q, q), q)
        got = nn(xbuf[0], pc[pl.ds(0, w), cc])
        for o in range(1, NZ):
            got = got + nn(xbuf[o], pc[pl.ds(o * w, w), cc])
        cond[:, cc] = got.astype(BF16)
        return 0

    with jax.named_scope("build"):
        lax.fori_loop(0, 2 * hw // BLK, build, 0)
    xbuf[z] = x_ref[...]
    load_lift.wait()
    lax.fori_loop(0, hw // BLK, mask_lift, 0)
    spread(z)
    spread(zr(-1))
    with jax.named_scope("barrier"):
        pl.semaphore_wait(bar, NZ - 1 + NR * NR - 1 + 1)
    ag_start(0, xbuf, x_ref)

    @pl.when(core == 1)
    def _():
        for e in (0, 1):
            dest = lax.rem(2 * z + e, NZ)
            piece = cot_ref.at[:, pl.ds(e * q, q)]
            land = cbuf.at[:, pl.ds(al((z // 4) * q, q), q)]

            @pl.when(dest != z)
            def _():
                remote(piece, land, cs.at[e], cr.at[z // 4], tensor=dest).start()

            @pl.when(dest == z)
            def _():
                cbuf[:, pl.ds(al((z // 4) * q, q), q)] = cot_ref[:, pl.ds(e * q, q)]

    spread(zr(1))
    pre[...] = times(z)
    spread(zr(-2))
    spread(zr(2))
    load_proj.wait()
    with jax.named_scope("mask_proj"):
        lax.fori_loop(0, 2 * hw // BLK, mask_proj, 0)
    for s in range(4):
        with jax.named_scope(f"agx{s}"):
            came = ag_step(0, xbuf, x_ref, s)
        if s < 3:
            spread((zr(-3), zr(3), zr(4))[s])
        for origin in came:
            pre[...] += times(origin)

    ring_sent(ag_s, ag_r)

    squash = jax.nn.sigmoid(pre[...])
    slope[...] = squash * (1.0 + pre[...] * (1.0 - squash))
    hid_ref[y, x] = (pre[...] * squash).astype(BF16)
    xy_tick(0, hid_ref, 0)

    hidden = hid_ref[y, x]

    def proj_rows(d, k):
        return pl.ds(al(k * hw + d * q, q), q)

    def shared_part(d):
        return jnp.concatenate(
            [nt(hidden, proj[proj_rows(d, 0), :]), nt(hidden, proj[proj_rows(d, 1), :])], axis=1
        )

    def shared_tick(s):
        if s == 1:
            got = nn(xbuf[0], m[pl.ds(0, w), pl.ds(w + q, q)])
            for o in range(1, NZ):
                got = got + nn(xbuf[o], m[pl.ds(o * w, w), pl.ds(w + q, q)])
            sm[:, pl.ds(q, q)] = got

    with jax.named_scope("rs_shared"):
        shared = rs(0, shared_part, shared_tick)()
    ring_sent(rs_s, rs_r)
    raw = shared[:, :q] + 2.0
    scale = jax.nn.sigmoid(raw)
    sm[:, pl.ds(0, q)] = scale
    sm[:, pl.ds(q, q)] += shared[:, q:]
    logs = jnp.minimum(raw, 0.0) - jnp.log1p(jnp.exp(-jnp.abs(raw)))
    logs = jnp.sum(logs.reshape(tok // 8, 8, q), axis=0)
    vec[1] = logs[:, :BLK] + logs[:, BLK:]
    xy_tick(0, hid_ref, 1)

    def cond_copy(o):
        oy, ox = o // NR, o % NR
        ty, tx = lax.rem(y + oy, NR), lax.rem(x + ox, NR)
        return remote(
            cond.at[:, pl.ds(al((ty * NR + tx) * BLK, BLK), BLK)],
            condc_ref.at[me],
            a_s,
            a_r,
            dp_0=ty,
            dp_1=tx,
        )

    def all_of(buf, ssem, rsem):
        ref = buf.at[pl.ds(0, buf.shape[0] - 1)]
        return remote(ref, ref, ssem, rsem, dp_0=lax.rem(y + 1, NR))

    def permute_tokens(lo, hi):
        with jax.named_scope("permute"):
            lax.fori_loop(lo, hi, pick, 0)
        if hi == hw // q:
            for o in range(1, NR * NR):
                cond_copy(o).start()
            condc_ref[me] = cond[:, pl.ds(al(me * BLK, BLK), BLK)]

    @pl.when(core == 1)
    def _():
        for k in (0, 1):

            @pl.when(4 * k + z // 2 != z)
            def _():
                ref = cbuf.at[:, pl.ds(k * q, q)]
                remote(ref, ref, cs.at[0], cr.at[k], tensor=z).wait_recv()

        cown[...] = cbuf[...]

    @pl.when(core == 0)
    def _():
        permute_tokens(0, hw // q)
        with jax.named_scope("handwait"):
            remote(gbuf, c0buf, hs, hr, layers=1 - core).wait_recv()
        cown[...] = c0buf[...]

    ca = cown[:, pl.ds(0, q)]
    cb = cown[:, pl.ds(q, q)].astype(F32)
    scale = sm[:, pl.ds(0, q)]
    keep_part = 1.0 - scale
    shift_grad = (cb * scale).astype(BF16)
    raw_grad = (cb * sm[:, pl.ds(q, q)] * scale * keep_part - keep_part).astype(BF16)
    stbuf[z, :, pl.ds(0, q)] = raw_grad
    stbuf[z, :, pl.ds(q, q)] = shift_grad
    own_st = stbuf.at[z]
    ag_start(1, stbuf, own_st)

    def st_copy(origin, k):
        to = origin + NZ * k
        return remote(
            stbuf.at[origin, :, pl.ds(k * q, q)],
            stc_ref.at[me],
            ts,
            tr,
            dp_0=to // NR,
            dp_1=lax.rem(to, NR),
        )

    def st_send(origin):
        for k in (0, 1):

            @pl.when(origin + NZ * k != me)
            def _():
                st_copy(origin, k).start()

            @pl.when(origin + NZ * k == me)
            def _():
                stc_ref[me] = stbuf[origin, :, pl.ds(k * q, q)]

    def act(origin):
        return nn(stbuf[origin, :, pl.ds(0, q)], proj[proj_rows(origin, 0), :]) + nn(
            stbuf[origin, :, pl.ds(q, q)], proj[proj_rows(origin, 1), :]
        )

    pre[...] = act(z)
    st_send(z)

    @pl.when(core == 1)
    def _():
        permute_tokens(0, 5)

    for s in range(4):
        with jax.named_scope(f"agst{s}"):
            came = ag_step(1, stbuf, own_st, s)
        if s < 2:
            for origin in came:
                st_send(origin)
        for origin in came:
            pre[...] += act(origin)
        if s == 0:

            @pl.when(core == 1)
            def _():
                permute_tokens(5, hw // q)

        if s == 0:

            @pl.when(core == 0)
            def _():
                xy_tick(0, hid_ref, 2)

        if s == 2:

            @pl.when(core == 1)
            def _():
                xy_tick(0, hid_ref, 2)

    grad_pre = (pre[...] * slope[...]).astype(BF16)
    gp_ref[y, x] = grad_pre
    xy_tick(1, gp_ref, 0)

    lhs = jnp.concatenate([grad_pre, ca, shift_grad], axis=1)

    def in_rows(d, k):
        there = jnp.where(core == 1, k * hw + d * q, (2 * d + k) * q)
        return pl.ds(al(there, q), q)

    def in_part(d):
        return jnp.concatenate([nt(lhs, m[in_rows(d, 0), :]), nt(lhs, m[in_rows(d, 1), :])], axis=1)

    def in_tick(s):
        if s < 3:

            @pl.when(core == 0)
            def _():
                xy_tick(1, gp_ref, s)

        if s == 1:
            for i in (-3, 3, 4):
                st_send(zr(i))

    with jax.named_scope("rs_in"):
        end = rs(1, in_part, in_tick)

    def gsend(k):
        return remote(
            cown.at[:, pl.ds(k * q, q)],
            gbuf.at[:, pl.ds(al(lax.rem(z, 2) * q, q), q)],
            gs.at[k],
            gr.at[lax.rem(z, 2)],
            tensor=4 * k + z // 2,
        )

    @pl.when(core == 1)
    def _():
        cown[...] = end().astype(BF16)
        remote(cown, c0buf, hs, hr, layers=1 - core).start()
        for k in (0, 1):

            @pl.when(4 * k + z // 2 != z)
            def _():
                gsend(k).start()

            @pl.when(4 * k + z // 2 == z)
            def _():
                gbuf[:, pl.ds(al(lax.rem(z, 2) * q, q), q)] = cown[:, pl.ds(k * q, q)]

        xy_tick(1, gp_ref, 1)
        xy_tick(0, hid_ref, 3)
        xy_tick(1, gp_ref, 2)

    tokens = NR * NR * tok

    def squares(g):
        g = jnp.sum((g * g).reshape(g.shape[0] // 8, 8, w), axis=0)
        out = g[:, :BLK]
        for c in range(1, w // BLK):
            out = out + g[:, c * BLK : (c + 1) * BLK]
        return out

    @pl.when(core == 0)
    def _():
        xy_tick(0, hid_ref, 3)

    with jax.named_scope("stcome"):
        all_of(stc_ref, ts, tr).wait_recv()
    with jax.named_scope("pgrad"):
        pgrad_ref[...] = tn(stc_ref[...].reshape(tokens, q), hid_ref[...].reshape(tokens, w))
    for b in range(q // BLK):
        for c in range(w // BLK):
            keep = pmask_ref[c, me * (q // BLK) + b].astype(F32)
            pgrad_ref[pl.ds(b * BLK, BLK), pl.ds(c * BLK, BLK)] *= keep
    vec[0] = squares(pgrad_ref[...])
    with jax.named_scope("condwait"):
        all_of(condc_ref, a_s, a_r).wait_recv()
    xy_tick(1, gp_ref, 3)
    with jax.named_scope("lgrad"):
        lgrad_ref[...] = tn(condc_ref[...].reshape(tokens, BLK), gp_ref[...].reshape(tokens, w))
    for c in range(w // BLK):
        keep = lmask_ref[c, me].astype(F32)
        lgrad_ref[:, pl.ds(c * BLK, BLK)] *= keep
    vec[0] += squares(lgrad_ref[...])

    save_pgrad = pltpu.make_async_copy(pgrad_ref, pgrad_out, o_s.at[0])
    save_lgrad = pltpu.make_async_copy(lgrad_ref, lgrad_out, o_s.at[1])
    save_gin = pltpu.make_async_copy(gin_ref, gin_out, o_s.at[2])
    def zcopy(i):
        return remote(vec, zbuf.at[z], zs, zrv, tensor=zr(i))

    for i in range(1, NZ):
        zcopy(i).start()
    zbuf[z] = vec[...]
    save_pgrad.start()
    save_lgrad.start()

    @pl.when(core == 1)
    def _():
        for e in (0, 1):

            @pl.when(lax.rem(2 * z + e, NZ) != z)
            def _():
                ref = gbuf.at[:, pl.ds(e * q, q)]
                remote(ref, ref, gs.at[0], gr.at[e], tensor=z).wait_recv()

        gin_ref[...] = gbuf[...].astype(F32)

    @pl.when(core == 0)
    def _():
        gin_ref[...] = end()

    save_gin.start()
    with jax.named_scope("zsum"):
        all_of(zbuf, zs, zrv).wait_recv()
    mid[...] = jnp.sum(zbuf[...], axis=0)

    def pcopy(o):
        ty, tx = lax.rem(y + o // NR, NR), lax.rem(x + o % NR, NR)
        return remote(mid, pbuf.at[me], ps, prv, dp_0=ty, dp_1=tx)

    for o in range(1, NR * NR):
        pcopy(o).start()
    pbuf[me] = mid[...]
    @pl.when(core == 1)
    def _():
        remote(cown, c0buf, hs, hr, layers=1 - core).wait_send()
        for k in (0, 1):

            @pl.when(4 * k + z // 2 != z)
            def _():
                gsend(k).wait_send()

        for e in (0, 1):
            dest = lax.rem(2 * z + e, NZ)

            @pl.when(dest != z)
            def _():
                ref = cot_ref.at[:, pl.ds(e * q, q)]
                remote(ref, ref, cs.at[e], cr.at[0], tensor=dest).wait_send()

    all_of(condc_ref, a_s, a_r).wait_send()
    all_of(stc_ref, ts, tr).wait_send()
    ring_sent(ag_s, ag_r)
    ring_sent(rs_s, rs_r)
    xy_finish(0)
    xy_finish(1)
    save_pgrad.wait()
    save_lgrad.wait()
    save_gin.wait()
    all_of(zbuf, zs, zrv).wait_send()

    with jax.named_scope("psum"):
        all_of(pbuf, ps, prv).wait_recv()
    other[0] = jnp.sum(pbuf[...], axis=0)
    swap = remote(other.at[0], other.at[1], ls, lr, layers=1 - core)
    swap.start()

    all_of(pbuf, ps, prv).wait_send()
    with jax.named_scope("swap"):
        swap.wait_recv()
    stat_ref[0] = other[0, 0] + other[1, 0]
    stat_ref[1] = other[0, 1]
    swap.wait_send()


def token_side(x, cot, lift_w, proj_w, lmask, pmask, perm):
    tok, w = x.shape
    hw = lift_w.shape[0]
    feat = 2 * hw
    q = w // 2
    dma = pltpu.SemaphoreType.DMA
    vm = pl.BlockSpec(memory_space=pltpu.VMEM)
    sm = pl.BlockSpec(memory_space=pltpu.SMEM)
    hbm = pl.BlockSpec(memory_space=pl.ANY)
    n = NR * NR
    return pl.pallas_call(
        token_kernel,
        out_shape=(
            jax.ShapeDtypeStruct((tok, w), F32),
            jax.ShapeDtypeStruct((2, 8, BLK), F32),
            jax.ShapeDtypeStruct((BLK, w), F32),
            jax.ShapeDtypeStruct((q, w), F32),
        ),
        in_specs=[vm, vm, hbm, hbm, sm, sm, vm],
        out_specs=(hbm, vm, hbm, hbm),
        scratch_shapes=[
            pltpu.VMEM((NZ, tok, w), BF16),
            pltpu.VMEM((feat, hw), BF16),
            pltpu.VMEM((feat, 2 * w), BF16),
            pltpu.VMEM((hw, w), BF16),
            pltpu.VMEM((feat, w), BF16),
            pltpu.VMEM((tok, hw), BF16),
            pltpu.VMEM((tok, w), F32),
            pltpu.VMEM((tok, w), F32),
            pltpu.VMEM((tok, w), F32),
            pltpu.VMEM((NZ, tok, w), BF16),
            pltpu.VMEM((2, 2, 4, tok, w), BF16),
            pltpu.VMEM((2, 2, 4, tok, w), BF16),
            pltpu.VMEM((tok, w), BF16),
            pltpu.VMEM((tok, w), BF16),
            pltpu.VMEM((tok, w), BF16),
            pltpu.VMEM((tok, w), BF16),
            pltpu.VMEM((n, tok, BLK), BF16),
            pltpu.VMEM((n, tok, q), BF16),
            pltpu.VMEM((NR, NR, tok, w), BF16),
            pltpu.VMEM((NR, NR, tok, w), BF16),
            pltpu.VMEM((2, 8, BLK), F32),
            pltpu.VMEM((NZ, 2, 8, BLK), F32),
            pltpu.VMEM((2, 8, BLK), F32),
            pltpu.VMEM((n, 2, 8, BLK), F32),
            pltpu.VMEM((2, 2, 8, BLK), F32),
            pltpu.VMEM((tok, w), F32),
            pltpu.VMEM((BLK, w), F32),
            pltpu.VMEM((q, w), F32),
            dma((2,)),
            dma((3,)),
            dma,
            dma((2, 4, NQ)),
            dma,
            dma((2, 4, NQ)),
            dma((2,)),
            dma((2,)),
            dma((2,)),
            dma((2,)),
            dma,
            dma,
            dma,
            dma,
            dma,
            dma,
            dma((2,)),
            dma((2, 2, 2, 2, 2)),
            dma,
            dma,
            dma,
            dma,
            dma,
            dma,
        ],
        compiler_params=pltpu.CompilerParams(
            collective_id=0, has_side_effects=True, vmem_limit_bytes=64 * 1024 * 1024 - 64 * 1024
        ),
        name="token_side",
    )(x, cot, lift_w, proj_w, lmask, pmask, perm)


def adam_kernel(
    lmask_ref,
    pmask_ref,
    stat_ref,
    lgrad_hbm,
    lmom_hbm,
    lsq_hbm,
    pgrad_hbm,
    pmom_hbm,
    psq_hbm,
    gin_hbm,
    lfirst_out,
    lsecond_out,
    lupdate_out,
    pfirst_out,
    psecond_out,
    pupdate_out,
    gin_out,
    log_ref,
    gin,
    grads,
    moms,
    sqs,
    news,
    in_s,
    out_s,
    gin_s,
    *,
    entries,
):
    me = lax.axis_index("dp_0") * NR + lax.axis_index("dp_1")
    n, rows, w = grads.shape
    blocks = []
    for b in range(n):
        r = pl.ds((b - 1) * rows, rows)
        if b == 0:
            ins = [lgrad_hbm, lmom_hbm.at[0], lsq_hbm.at[0]]
            outs = [lfirst_out.at[0], lsecond_out.at[0], lupdate_out.at[0]]
        else:
            ins = [pgrad_hbm.at[r], pmom_hbm.at[0, r], psq_hbm.at[0, r]]
            outs = [pfirst_out.at[0, r], psecond_out.at[0, r], pupdate_out.at[0, r]]
        loads = [
            pltpu.make_async_copy(ref, buf.at[b], in_s.at[b, k])
            for k, (ref, buf) in enumerate(zip(ins, (grads, moms, sqs)))
        ]
        saves = [pltpu.make_async_copy(news.at[b, k], ref, out_s.at[b, k]) for k, ref in enumerate(outs)]
        blocks.append((loads, saves))
    for loads, _ in blocks:
        for c in loads:
            c.start()
    gin_load = pltpu.make_async_copy(gin_hbm, gin, gin_s.at[0])
    gin_save = pltpu.make_async_copy(gin, gin_out.at[0], gin_s.at[1])
    gin_load.start()
    total = jnp.sum(stat_ref[0], keepdims=True)
    factor = jnp.minimum(1.0, CLIP / (jnp.sqrt(total) + 1e-06))
    log_ref[0] = jnp.sum(stat_ref[1]) * (1.0 / entries)
    bias_one = 1.0 - beta_one**ADAM_STEP
    bias_two = 1.0 - beta_two**ADAM_STEP
    for b, (loads, saves) in enumerate(blocks):
        for c in loads:
            c.wait()
        for c in range(w // BLK):
            cc = pl.ds(c * BLK, BLK)
            keep = (lmask_ref[c, me] if b == 0 else pmask_ref[c, me * (n - 1) + b - 1]) > 0
            moment = moms[b, :, cc]
            square = sqs[b, :, cc]
            scaled = grads[b, :, cc] * factor
            first = jnp.where(keep, beta_one * moment + (1.0 - beta_one) * scaled, moment)
            second = jnp.where(keep, beta_two * square + (1.0 - beta_two) * scaled * scaled, square)
            update = (first * (1.0 / bias_one)) / (jnp.sqrt(second * (1.0 / bias_two)) + adam_eps)
            news[b, 0, :, cc] = first
            news[b, 1, :, cc] = second
            news[b, 2, :, cc] = jnp.where(keep, update, 0.0)
        for c in saves:
            c.start()
    gin_load.wait()
    gin_save.start()
    gin_save.wait()
    for _, saves in blocks:
        for c in saves:
            c.wait()


def adam(entries, lmask, pmask, stat, lgrad, lmom, lsq, pgrad, pmom, psq, gin):
    dma = pltpu.SemaphoreType.DMA
    vm = pl.BlockSpec(memory_space=pltpu.VMEM)
    smem = pl.BlockSpec(memory_space=pltpu.SMEM)
    hbm = pl.BlockSpec(memory_space=pl.ANY)
    rows, w = lgrad.shape
    n = 1 + pgrad.shape[0] // rows
    like = jax.ShapeDtypeStruct
    return pl.pallas_call(
        functools.partial(adam_kernel, entries=entries),
        out_shape=(like(lmom.shape, F32),) * 3
        + (like(pmom.shape, F32),) * 3
        + (like((1,) + gin.shape, F32), like((1,), F32)),
        in_specs=[smem, smem, vm] + [hbm] * 7,
        out_specs=(hbm,) * 7 + (smem,),
        scratch_shapes=[
            pltpu.VMEM(gin.shape, F32),
            pltpu.VMEM((n, rows, w), F32),
            pltpu.VMEM((n, rows, w), F32),
            pltpu.VMEM((n, rows, w), F32),
            pltpu.VMEM((n, 3, rows, w), F32),
            dma((n, 3)),
            dma((n, 3)),
            dma((2,)),
        ],
        name="adam",
    )(lmask, pmask, stat, lgrad, lmom, lsq, pgrad, pmom, psq, gin)


def per_device(
    section_input,
    out_cotangent,
    lift_weight,
    proj_weight,
    lift_mask,
    proj_mask,
    channel_perm,
    lift_moment,
    lift_square,
    proj_moment,
    proj_square,
):
    lmask, pmask = lift_mask[0].T, proj_mask[0].T
    gin, stat, lift_grad, proj_grad = token_side(
        section_input[0], out_cotangent, lift_weight[0], proj_weight[0], lmask, pmask, channel_perm
    )
    tokens = NR * NR * gin.shape[0]
    *stepped, input_grad, log_det = adam(
        tokens * lift_weight.shape[1],
        lmask,
        pmask,
        stat,
        lift_grad,
        lift_moment,
        lift_square,
        proj_grad,
        proj_moment,
        proj_square,
        gin,
    )
    return (input_grad, log_det) + tuple(stepped)


def solution(mesh):
    finer = Mesh(
        mesh.devices.reshape(NR, NR, mesh.shape["tensor"], mesh.shape["layers"]),
        ("dp_0", "dp_1", "tensor", "layers"),
    )
    tiled = P("layers", DP, "tensor")
    weight = P("layers", None, "tensor")
    return jax.shard_map(
        per_device,
        mesh=finer,
        in_specs=(tiled, P(DP, "tensor")) + (weight,) * 4 + (P("layers", None),) + (tiled,) * 4,
        out_specs=(tiled, P("layers")) + (tiled,) * 6,
        check_vma=False,
    )
```

```python
import functools

import jax
import jax.numpy as jnp
from jax import lax
from jax.experimental import pallas as pl
from jax.experimental.pallas import tpu as pltpu
from jax.sharding import Mesh
from jax.sharding import PartitionSpec as P

BLK = 128
ADAM_STEP = 10
CLIP = 4096
DP = ("dp_0", "dp_1")
MESH = pl.DeviceIdType.MESH
F32 = jnp.float32
BF16 = jnp.bfloat16

NZ = 8
NR = 4
NQ = 4

beta_one = 0.9
beta_two = 0.99
adam_eps = 1e-08


def nn(a, b):
    return jnp.dot(a, b, preferred_element_type=F32)


def nt(a, b):
    return lax.dot_general(a, b, (((1,), (1,)), ((), ())), preferred_element_type=F32)


def tn(a, b):
    return lax.dot_general(a, b, (((0,), (0,)), ((), ())), preferred_element_type=F32)


def al(i, m):
    return pl.multiple_of(i, m)


def remote(src, dst, ssem, rsem, **where):
    return pltpu.make_async_remote_copy(
        src_ref=src, dst_ref=dst, send_sem=ssem, recv_sem=rsem, device_id=where, device_id_type=MESH
    )


def far(d, h):
    return (h < NQ // 2) == (d == 0)


def both_ways(d, s, h):
    return s < 3 or far(d, h)


FIRST = [sorted(range(NQ), key=lambda h: not far(d, h)) for d in (0, 1)]
LAST = [sorted(range(NQ), key=lambda h: far(d, h)) for d in (0, 1)]


def token_kernel(
    x_ref,
    cot_ref,
    lift_hbm,
    proj_hbm,
    lmask_ref,
    pmask_ref,
    perm_ref,
    gin_out,
    stat_ref,
    lgrad_out,
    pgrad_out,
    xbuf,
    pc,
    m,
    lift,
    proj,
    cond,
    sm,
    slope,
    pre,
    stbuf,
    sbuf,
    rbuf,
    cbuf,
    c0buf,
    gbuf,
    cown,
    condc_ref,
    stc_ref,
    hid_ref,
    gp_ref,
    vec,
    zbuf,
    mid,
    pbuf,
    other,
    gin_ref,
    lgrad_ref,
    pgrad_ref,
    w_s,
    o_s,
    ag_s,
    ag_r,
    rs_s,
    rs_r,
    cs,
    cr,
    gs,
    gr,
    hs,
    hr,
    a_s,
    a_r,
    ts,
    tr,
    xs,
    xr,
    zs,
    zrv,
    ps,
    prv,
    ls,
    lr,
):
    z = lax.axis_index("tensor")
    y = lax.axis_index("dp_0")
    x = lax.axis_index("dp_1")
    core = lax.axis_index("layers")
    me = y * NR + x
    tok = x_ref.shape[0]
    half = tok // 2
    quart = tok // 4
    w = x_ref.shape[1]
    q = w // 2
    hw = NZ * q

    nq = tok // NQ

    def rows(h):
        return pl.ds(h * nq, nq)

    def zr(i):
        return lax.rem(z + NZ + i, NZ)

    zside = (zr(1), zr(-1))
    load_lift = pltpu.make_async_copy(lift_hbm, lift, w_s.at[0])
    load_proj = pltpu.make_async_copy(proj_hbm, proj, w_s.at[1])
    load_lift.start()
    load_proj.start()

    bar = pltpu.get_barrier_semaphore()
    for i in range(1, NZ):
        pl.semaphore_signal(bar, inc=1, device_id={"tensor": zr(i)}, device_id_type=MESH)
    for oy in range(NR):
        for ox in range(NR):
            if oy or ox:
                pl.semaphore_signal(
                    bar,
                    inc=1,
                    device_id={"dp_0": lax.rem(y + oy, NR), "dp_1": lax.rem(x + ox, NR)},
                    device_id_type=MESH,
                )
    pl.semaphore_signal(bar, inc=1, device_id={"layers": 1 - core}, device_id_type=MESH)

    def ag_copy(p, buf, own, s, d, h):
        origin = zr(-s) if d == 0 else zr(s)
        src = own.at[rows(h)] if s == 0 else buf.at[origin, rows(h)]
        return remote(src, buf.at[origin, rows(h)], ag_s, ag_r.at[d, s, h], tensor=zside[d])

    def ag_wait(p, buf, s, d, h):
        origin = zr(-1 - s) if d == 0 else zr(1 + s)
        ref = buf.at[origin, rows(h)]
        remote(ref, ref, ag_s, ag_r.at[d, s, h], tensor=zside[d]).wait_recv()

    def ag_start(p, buf, own):
        for k in range(NQ):
            for d in (0, 1):
                ag_copy(p, buf, own, 0, d, FIRST[d][k]).start()

    def ag_step(p, buf, own, s):
        for k in range(NQ):
            for d in (0, 1):
                h = FIRST[d][k]
                if both_ways(d, s, h):
                    ag_wait(p, buf, s, d, h)
                    if s < 3 and both_ways(d, s + 1, h):
                        ag_copy(p, buf, own, s + 1, d, h).start()
        return [zr(-1 - s), zr(1 + s)] if s < 3 else [zr(4)]

    def ring_sent(ssem, rsem):
        ref = xbuf.at[pl.ds(0, NZ - 1)]
        remote(ref, ref, ssem, rsem.at[0, 0, 0], tensor=zside[0]).wait_send()

    def rs_copy(p, s, d, h):
        return remote(
            sbuf.at[p, d, s, rows(h)],
            rbuf.at[p, d, s, rows(h)],
            rs_s,
            rs_r.at[d, s, h],
            tensor=zside[d],
        )

    def rs(p, part, tick):
        most = part(zr(4))
        for k in range(NQ // 2):
            for d in (0, 1):
                h = FIRST[d][k]
                sbuf[p, d, 0, rows(h)] = most[h * nq : (h + 1) * nq].astype(BF16)
                rs_copy(p, 0, d, h).start()
        for s in (1, 2, 3):
            mine = [part(zr(4 - s)), part(zr(s - 4))]

            def send(d, h, own):
                sbuf[p, d, s, rows(h)] = own.astype(BF16)
                rs_copy(p, s, d, h).start()

            if s == 1:
                for k in range(NQ // 2):
                    for d in (0, 1):
                        h = LAST[d][k]
                        send(d, h, mine[d][h * nq : (h + 1) * nq])
            with jax.named_scope(f"tick{s}"):
                tick(s)
            with jax.named_scope(f"w{s}"):
                for k in range(NQ // 2 if s == 1 else 0, NQ):
                    for d in (0, 1):
                        h = LAST[d][k]
                        rs_copy(p, s - 1, d, h).wait_recv()
                        own = mine[d][h * nq : (h + 1) * nq]
                        send(d, h, own + rbuf[p, d, s - 1, rows(h)].astype(F32))

        def end():
            own = part(z)
            with jax.named_scope("w4"):
                for d in (0, 1):
                    for h in range(NQ):
                        rs_copy(p, 3, d, h).wait_recv()
            return own + rbuf[p, 0, 3].astype(F32) + rbuf[p, 1, 3].astype(F32)

        return end

    def along(axis, i):
        if axis == "dp_1":
            return {"dp_1": lax.rem(x + NR + i, NR)}
        return {"dp_0": lax.rem(y + NR + i, NR)}

    def slot(buf, stage, h, off, r):
        axis = ("dp_1", "dp_0")[(h + stage) % 2]
        yy, xx = (y, lax.rem(x + NR + off, NR)) if axis == "dp_1" else (lax.rem(y + NR + off, NR), x)
        if stage == 0:
            return buf.at[yy, xx, r]
        return buf.at[yy, :, r] if axis == "dp_0" else buf.at[:, xx, r]

    def xy_rows(h, t, d):
        if t == 0:
            return pl.ds(h * half, half)
        return pl.ds(h * half + d * quart, quart)

    def xy_copy(p, buf, stage, h, t, d):
        axis = ("dp_1", "dp_0")[(h + stage) % 2]
        step = 1 if d == 0 else -1
        off = 0 if t == 0 else -step
        rr = xy_rows(h, t, d)
        if stage == 0 and t == 1:
            step, off, rr = 2, 0, xy_rows(h, 0, 0)
        src = slot(buf, stage, h, off, rr)
        return remote(src, src, xs.at[p], xr.at[p, stage, h, t, d], **along(axis, step))

    def xy_wait(p, buf, stage, h, t, d):
        step = 1 if d == 0 else -1
        off = -step if t == 0 else -2 * step
        rr = xy_rows(h, 0 if stage == 0 else t, d)
        ref = slot(buf, stage, h, off, rr)
        remote(ref, ref, xs.at[p], xr.at[p, stage, h, t, d], tensor=zside[0]).wait_recv()

    def xy_each(stage, t, act_on):
        for h in (0, 1):
            for d in (0,) if stage == 0 and t == 1 else (0, 1):
                act_on(stage, h, t, d)

    def xy_tick(p, buf, k):
        with jax.named_scope(f"xy{p}{k}"):
            for stage, t in ((), ((0, 0), (0, 1)), ((1, 0),), ((1, 1),))[k]:
                xy_each(stage, t, lambda *a: xy_wait(p, buf, *a))
            for stage, t in (((0, 0), (0, 1)), ((1, 0),), ((1, 1),), ())[k]:
                xy_each(stage, t, lambda *a: xy_copy(p, buf, *a).start())

    def xy_finish(p):
        ref = m.at[pl.ds(0, (NR * NR - 1) * tok // 2)]
        remote(ref, ref, xs.at[p], xr.at[p, 0, 0, 0, 0], tensor=zside[0]).wait_send()

    def mask_lift(i, _):
        r = pl.ds(al(i * BLK, BLK), BLK)
        for c in range(w // BLK):
            cc = pl.ds(c * BLK, BLK)
            keep = lmask_ref[c, i].astype(F32)
            lift[r, cc] = (lift[r, cc].astype(F32) * keep).astype(BF16)
        return 0

    def mask_proj(i, _):
        r = pl.ds(al(i * BLK, BLK), BLK)
        for c in range(w // BLK):
            cc = pl.ds(c * BLK, BLK)
            keep = pmask_ref[c, i].astype(F32)
            proj[r, cc] = (proj[r, cc].astype(F32) * keep).astype(BF16)
        return 0

    ca_perm = pl.ds(al(z * q, q), q)
    mv_perm = pl.ds(al(hw + z * q, q), q)

    def hot(base, order):
        at = lax.broadcasted_iota(jnp.int32, (BLK, q), 0) + base
        return jnp.where(at == order, 1.0, 0.0).astype(BF16)

    def build(i, _):
        base = i * BLK
        r = pl.ds(al(base, BLK), BLK)
        for c in range(hw // q):
            cc = pl.ds(c * q, q)
            pc[r, cc] = hot(base, perm_ref[:, cc])
        m[r, pl.ds(w, q)] = hot(base, perm_ref[:, ca_perm])
        m[r, pl.ds(w + q, q)] = hot(base, perm_ref[:, mv_perm])
        return 0

    def of(origin):
        return pl.ds(al(origin * w, w), w)

    def spread(origin):
        with jax.named_scope("spread"):
            m[of(origin), pl.ds(0, w)] = nn(pc[of(origin), :], lift[...]).astype(BF16)

    def times(origin):
        return nn(xbuf[origin], m[of(origin), pl.ds(0, w)])

    def pick(c, _):
        cc = pl.ds(al(c * q, q), q)
        got = nn(xbuf[0], pc[pl.ds(0, w), cc])
        for o in range(1, NZ):
            got = got + nn(xbuf[o], pc[pl.ds(o * w, w), cc])
        cond[:, cc] = got.astype(BF16)
        return 0

    with jax.named_scope("build"):
        lax.fori_loop(0, 2 * hw // BLK, build, 0)
    xbuf[z] = x_ref[...]
    load_lift.wait()
    lax.fori_loop(0, hw // BLK, mask_lift, 0)
    spread(z)
    spread(zr(-1))
    with jax.named_scope("barrier"):
        pl.semaphore_wait(bar, NZ - 1 + NR * NR - 1 + 1)

    @pl.when(core == 1)
    def _():
        ag_start(0, xbuf, x_ref)
        for e in (0, 1):
            dest = lax.rem(2 * z + e, NZ)
            piece = cot_ref.at[:, pl.ds(e * q, q)]
            land = cbuf.at[:, pl.ds(al((z // 4) * q, q), q)]

            @pl.when(dest != z)
            def _():
                remote(piece, land, cs.at[e], cr.at[z // 4], tensor=dest).start()

            @pl.when(dest == z)
            def _():
                cbuf[:, pl.ds(al((z // 4) * q, q), q)] = cot_ref[:, pl.ds(e * q, q)]

    spread(zr(1))
    pre[...] = times(z)
    spread(zr(-2))
    spread(zr(2))
    load_proj.wait()
    with jax.named_scope("mask_proj"):
        lax.fori_loop(0, 2 * hw // BLK, mask_proj, 0)

    @pl.when(core == 0)
    def _():
        ag_start(0, xbuf, x_ref)

    for s in range(4):
        with jax.named_scope(f"agx{s}"):
            came = ag_step(0, xbuf, x_ref, s)
        if s < 3:
            spread((zr(-3), zr(3), zr(4))[s])
        for origin in came:
            pre[...] += times(origin)

    ring_sent(ag_s, ag_r)

    squash = jax.nn.sigmoid(pre[...])
    slope[...] = squash * (1.0 + pre[...] * (1.0 - squash))
    hid_ref[y, x] = (pre[...] * squash).astype(BF16)
    xy_tick(0, hid_ref, 0)

    hidden = hid_ref[y, x]

    def proj_rows(d, k):
        return pl.ds(al(k * hw + d * q, q), q)

    def shared_part(d):
        return jnp.concatenate(
            [nt(hidden, proj[proj_rows(d, 0), :]), nt(hidden, proj[proj_rows(d, 1), :])], axis=1
        )

    def shared_tick(s):
        if s == 1:
            got = nn(xbuf[0], m[pl.ds(0, w), pl.ds(w + q, q)])
            for o in range(1, NZ):
                got = got + nn(xbuf[o], m[pl.ds(o * w, w), pl.ds(w + q, q)])
            sm[:, pl.ds(q, q)] = got

    with jax.named_scope("rs_shared"):
        shared = rs(0, shared_part, shared_tick)()
    ring_sent(rs_s, rs_r)
    raw = shared[:, :q] + 2.0
    scale = jax.nn.sigmoid(raw)
    sm[:, pl.ds(0, q)] = scale
    sm[:, pl.ds(q, q)] += shared[:, q:]
    logs = jnp.minimum(raw, 0.0) - jnp.log1p(jnp.exp(-jnp.abs(raw)))
    logs = jnp.sum(logs.reshape(tok // 8, 8, q), axis=0)
    vec[1] = logs[:, :BLK] + logs[:, BLK:]
    xy_tick(0, hid_ref, 1)

    def cond_copy(o):
        oy, ox = o // NR, o % NR
        ty, tx = lax.rem(y + oy, NR), lax.rem(x + ox, NR)
        return remote(
            cond.at[:, pl.ds(al((ty * NR + tx) * BLK, BLK), BLK)],
            condc_ref.at[me],
            a_s,
            a_r,
            dp_0=ty,
            dp_1=tx,
        )

    def all_of(buf, ssem, rsem):
        ref = buf.at[pl.ds(0, buf.shape[0] - 1)]
        return remote(ref, ref, ssem, rsem, dp_0=lax.rem(y + 1, NR))

    def permute_tokens(lo, hi):
        with jax.named_scope("permute"):
            lax.fori_loop(lo, hi, pick, 0)
        if hi == hw // q:
            for o in range(1, NR * NR):
                cond_copy(o).start()
            condc_ref[me] = cond[:, pl.ds(al(me * BLK, BLK), BLK)]

    @pl.when(core == 1)
    def _():
        for k in (0, 1):

            @pl.when(4 * k + z // 2 != z)
            def _():
                ref = cbuf.at[:, pl.ds(k * q, q)]
                remote(ref, ref, cs.at[0], cr.at[k], tensor=z).wait_recv()

        cown[...] = cbuf[...]

    @pl.when(core == 0)
    def _():
        permute_tokens(0, hw // q)
        with jax.named_scope("handwait"):
            remote(gbuf, c0buf, hs, hr, layers=1 - core).wait_recv()
        cown[...] = c0buf[...]

    ca = cown[:, pl.ds(0, q)]
    cb = cown[:, pl.ds(q, q)].astype(F32)
    scale = sm[:, pl.ds(0, q)]
    keep_part = 1.0 - scale
    shift_grad = (cb * scale).astype(BF16)
    raw_grad = (cb * sm[:, pl.ds(q, q)] * scale * keep_part - keep_part).astype(BF16)
    stbuf[z, :, pl.ds(0, q)] = raw_grad
    stbuf[z, :, pl.ds(q, q)] = shift_grad
    own_st = stbuf.at[z]
    ag_start(1, stbuf, own_st)

    def st_copy(origin, k):
        to = origin + NZ * k
        return remote(
            stbuf.at[origin, :, pl.ds(k * q, q)],
            stc_ref.at[me],
            ts,
            tr,
            dp_0=to // NR,
            dp_1=lax.rem(to, NR),
        )

    def st_send(origin):
        for k in (0, 1):

            @pl.when(origin + NZ * k != me)
            def _():
                st_copy(origin, k).start()

            @pl.when(origin + NZ * k == me)
            def _():
                stc_ref[me] = stbuf[origin, :, pl.ds(k * q, q)]

    def act(origin):
        return nn(stbuf[origin, :, pl.ds(0, q)], proj[proj_rows(origin, 0), :]) + nn(
            stbuf[origin, :, pl.ds(q, q)], proj[proj_rows(origin, 1), :]
        )

    pre[...] = act(z)
    st_send(z)

    @pl.when(core == 1)
    def _():
        permute_tokens(0, 5)

    for s in range(4):
        with jax.named_scope(f"agst{s}"):
            came = ag_step(1, stbuf, own_st, s)
        if s < 2:
            for origin in came:
                st_send(origin)
        for origin in came:
            pre[...] += act(origin)
        if s == 0:

            @pl.when(core == 1)
            def _():
                permute_tokens(5, hw // q)

        if s == 0:

            @pl.when(core == 0)
            def _():
                xy_tick(0, hid_ref, 2)

        if s == 2:

            @pl.when(core == 1)
            def _():
                xy_tick(0, hid_ref, 2)

    grad_pre = (pre[...] * slope[...]).astype(BF16)
    gp_ref[y, x] = grad_pre
    xy_tick(1, gp_ref, 0)

    lhs = jnp.concatenate([grad_pre, ca, shift_grad], axis=1)

    def in_rows(d, k):
        there = jnp.where(core == 1, k * hw + d * q, (2 * d + k) * q)
        return pl.ds(al(there, q), q)

    def in_part(d):
        return jnp.concatenate([nt(lhs, m[in_rows(d, 0), :]), nt(lhs, m[in_rows(d, 1), :])], axis=1)

    def in_tick(s):
        if s == 1:

            @pl.when(core == 0)
            def _():
                xy_tick(1, gp_ref, 1)

            for i in (-3, 3, 4):
                st_send(zr(i))

    with jax.named_scope("rs_in"):
        end = rs(1, in_part, in_tick)

    def gsend(k):
        return remote(
            cown.at[:, pl.ds(k * q, q)],
            gbuf.at[:, pl.ds(al(lax.rem(z, 2) * q, q), q)],
            gs.at[k],
            gr.at[lax.rem(z, 2)],
            tensor=4 * k + z // 2,
        )

    @pl.when(core == 1)
    def _():
        cown[...] = end().astype(BF16)
        remote(cown, c0buf, hs, hr, layers=1 - core).start()
        for k in (0, 1):

            @pl.when(4 * k + z // 2 != z)
            def _():
                gsend(k).start()

            @pl.when(4 * k + z // 2 == z)
            def _():
                gbuf[:, pl.ds(al(lax.rem(z, 2) * q, q), q)] = cown[:, pl.ds(k * q, q)]

        xy_tick(1, gp_ref, 1)
        xy_tick(0, hid_ref, 3)
        xy_tick(1, gp_ref, 2)

    tokens = NR * NR * tok

    def squares(g):
        g = jnp.sum((g * g).reshape(g.shape[0] // 8, 8, w), axis=0)
        out = g[:, :BLK]
        for c in range(1, w // BLK):
            out = out + g[:, c * BLK : (c + 1) * BLK]
        return out

    @pl.when(core == 0)
    def _():
        xy_tick(0, hid_ref, 3)
        xy_tick(1, gp_ref, 2)

    with jax.named_scope("stcome"):
        all_of(stc_ref, ts, tr).wait_recv()
    with jax.named_scope("pgrad"):
        pgrad_ref[...] = tn(stc_ref[...].reshape(tokens, q), hid_ref[...].reshape(tokens, w))
    for b in range(q // BLK):
        for c in range(w // BLK):
            keep = pmask_ref[c, me * (q // BLK) + b].astype(F32)
            pgrad_ref[pl.ds(b * BLK, BLK), pl.ds(c * BLK, BLK)] *= keep
    vec[0] = squares(pgrad_ref[...])
    with jax.named_scope("condwait"):
        all_of(condc_ref, a_s, a_r).wait_recv()
    xy_tick(1, gp_ref, 3)
    with jax.named_scope("lgrad"):
        lgrad_ref[...] = tn(condc_ref[...].reshape(tokens, BLK), gp_ref[...].reshape(tokens, w))
    for c in range(w // BLK):
        keep = lmask_ref[c, me].astype(F32)
        lgrad_ref[:, pl.ds(c * BLK, BLK)] *= keep
    vec[0] += squares(lgrad_ref[...])

    save_pgrad = pltpu.make_async_copy(pgrad_ref, pgrad_out, o_s.at[0])
    save_lgrad = pltpu.make_async_copy(lgrad_ref, lgrad_out, o_s.at[1])
    save_gin = pltpu.make_async_copy(gin_ref, gin_out, o_s.at[2])
    def zcopy(i):
        return remote(vec, zbuf.at[z], zs, zrv, tensor=zr(i))

    for i in range(1, NZ):
        zcopy(i).start()
    zbuf[z] = vec[...]
    save_pgrad.start()
    save_lgrad.start()

    @pl.when(core == 1)
    def _():
        for e in (0, 1):

            @pl.when(lax.rem(2 * z + e, NZ) != z)
            def _():
                ref = gbuf.at[:, pl.ds(e * q, q)]
                remote(ref, ref, gs.at[0], gr.at[e], tensor=z).wait_recv()

        gin_ref[...] = gbuf[...].astype(F32)

    @pl.when(core == 0)
    def _():
        gin_ref[...] = end()

    save_gin.start()
    with jax.named_scope("zsum"):
        all_of(zbuf, zs, zrv).wait_recv()
    mid[...] = jnp.sum(zbuf[...], axis=0)

    def pcopy(o):
        ty, tx = lax.rem(y + o // NR, NR), lax.rem(x + o % NR, NR)
        return remote(mid, pbuf.at[me], ps, prv, dp_0=ty, dp_1=tx)

    for o in range(1, NR * NR):
        pcopy(o).start()
    pbuf[me] = mid[...]
    @pl.when(core == 1)
    def _():
        remote(cown, c0buf, hs, hr, layers=1 - core).wait_send()
        for k in (0, 1):

            @pl.when(4 * k + z // 2 != z)
            def _():
                gsend(k).wait_send()

        for e in (0, 1):
            dest = lax.rem(2 * z + e, NZ)

            @pl.when(dest != z)
            def _():
                ref = cot_ref.at[:, pl.ds(e * q, q)]
                remote(ref, ref, cs.at[e], cr.at[0], tensor=dest).wait_send()

    all_of(condc_ref, a_s, a_r).wait_send()
    all_of(stc_ref, ts, tr).wait_send()
    ring_sent(ag_s, ag_r)
    ring_sent(rs_s, rs_r)
    xy_finish(0)
    xy_finish(1)
    save_pgrad.wait()
    save_lgrad.wait()
    save_gin.wait()
    all_of(zbuf, zs, zrv).wait_send()

    with jax.named_scope("psum"):
        all_of(pbuf, ps, prv).wait_recv()
    other[0] = jnp.sum(pbuf[...], axis=0)
    swap = remote(other.at[0], other.at[1], ls, lr, layers=1 - core)
    swap.start()

    all_of(pbuf, ps, prv).wait_send()
    with jax.named_scope("swap"):
        swap.wait_recv()
    stat_ref[0] = other[0, 0] + other[1, 0]
    stat_ref[1] = other[0, 1]
    swap.wait_send()


def token_side(x, cot, lift_w, proj_w, lmask, pmask, perm):
    tok, w = x.shape
    hw = lift_w.shape[0]
    feat = 2 * hw
    q = w // 2
    dma = pltpu.SemaphoreType.DMA
    vm = pl.BlockSpec(memory_space=pltpu.VMEM)
    sm = pl.BlockSpec(memory_space=pltpu.SMEM)
    hbm = pl.BlockSpec(memory_space=pl.ANY)
    n = NR * NR
    return pl.pallas_call(
        token_kernel,
        out_shape=(
            jax.ShapeDtypeStruct((tok, w), F32),
            jax.ShapeDtypeStruct((2, 8, BLK), F32),
            jax.ShapeDtypeStruct((BLK, w), F32),
            jax.ShapeDtypeStruct((q, w), F32),
        ),
        in_specs=[vm, vm, hbm, hbm, sm, sm, vm],
        out_specs=(hbm, vm, hbm, hbm),
        scratch_shapes=[
            pltpu.VMEM((NZ, tok, w), BF16),
            pltpu.VMEM((feat, hw), BF16),
            pltpu.VMEM((feat, 2 * w), BF16),
            pltpu.VMEM((hw, w), BF16),
            pltpu.VMEM((feat, w), BF16),
            pltpu.VMEM((tok, hw), BF16),
            pltpu.VMEM((tok, w), F32),
            pltpu.VMEM((tok, w), F32),
            pltpu.VMEM((tok, w), F32),
            pltpu.VMEM((NZ, tok, w), BF16),
            pltpu.VMEM((2, 2, 4, tok, w), BF16),
            pltpu.VMEM((2, 2, 4, tok, w), BF16),
            pltpu.VMEM((tok, w), BF16),
            pltpu.VMEM((tok, w), BF16),
            pltpu.VMEM((tok, w), BF16),
            pltpu.VMEM((tok, w), BF16),
            pltpu.VMEM((n, tok, BLK), BF16),
            pltpu.VMEM((n, tok, q), BF16),
            pltpu.VMEM((NR, NR, tok, w), BF16),
            pltpu.VMEM((NR, NR, tok, w), BF16),
            pltpu.VMEM((2, 8, BLK), F32),
            pltpu.VMEM((NZ, 2, 8, BLK), F32),
            pltpu.VMEM((2, 8, BLK), F32),
            pltpu.VMEM((n, 2, 8, BLK), F32),
            pltpu.VMEM((2, 2, 8, BLK), F32),
            pltpu.VMEM((tok, w), F32),
            pltpu.VMEM((BLK, w), F32),
            pltpu.VMEM((q, w), F32),
            dma((2,)),
            dma((3,)),
            dma,
            dma((2, 4, NQ)),
            dma,
            dma((2, 4, NQ)),
            dma((2,)),
            dma((2,)),
            dma((2,)),
            dma((2,)),
            dma,
            dma,
            dma,
            dma,
            dma,
            dma,
            dma((2,)),
            dma((2, 2, 2, 2, 2)),
            dma,
            dma,
            dma,
            dma,
            dma,
            dma,
        ],
        compiler_params=pltpu.CompilerParams(
            collective_id=0, has_side_effects=True, vmem_limit_bytes=64 * 1024 * 1024 - 64 * 1024
        ),
        name="token_side",
    )(x, cot, lift_w, proj_w, lmask, pmask, perm)


def adam_kernel(
    lmask_ref,
    pmask_ref,
    stat_ref,
    lgrad_hbm,
    lmom_hbm,
    lsq_hbm,
    pgrad_hbm,
    pmom_hbm,
    psq_hbm,
    gin_hbm,
    lfirst_out,
    lsecond_out,
    lupdate_out,
    pfirst_out,
    psecond_out,
    pupdate_out,
    gin_out,
    log_ref,
    gin,
    grads,
    moms,
    sqs,
    news,
    in_s,
    out_s,
    gin_s,
    *,
    entries,
):
    me = lax.axis_index("dp_0") * NR + lax.axis_index("dp_1")
    n, rows, w = grads.shape
    blocks = []
    for b in range(n):
        r = pl.ds((b - 1) * rows, rows)
        if b == 0:
            ins = [lgrad_hbm, lmom_hbm.at[0], lsq_hbm.at[0]]
            outs = [lfirst_out.at[0], lsecond_out.at[0], lupdate_out.at[0]]
        else:
            ins = [pgrad_hbm.at[r], pmom_hbm.at[0, r], psq_hbm.at[0, r]]
            outs = [pfirst_out.at[0, r], psecond_out.at[0, r], pupdate_out.at[0, r]]
        loads = [
            pltpu.make_async_copy(ref, buf.at[b], in_s.at[b, k])
            for k, (ref, buf) in enumerate(zip(ins, (grads, moms, sqs)))
        ]
        saves = [pltpu.make_async_copy(news.at[b, k], ref, out_s.at[b, k]) for k, ref in enumerate(outs)]
        blocks.append((loads, saves))
    for loads, _ in blocks:
        for c in loads:
            c.start()
    gin_load = pltpu.make_async_copy(gin_hbm, gin, gin_s.at[0])
    gin_save = pltpu.make_async_copy(gin, gin_out.at[0], gin_s.at[1])
    gin_load.start()
    total = jnp.sum(stat_ref[0], keepdims=True)
    factor = jnp.minimum(1.0, CLIP / (jnp.sqrt(total) + 1e-06))
    log_ref[0] = jnp.sum(stat_ref[1]) * (1.0 / entries)
    bias_one = 1.0 - beta_one**ADAM_STEP
    bias_two = 1.0 - beta_two**ADAM_STEP
    for b, (loads, saves) in enumerate(blocks):
        for c in loads:
            c.wait()
        for c in range(w // BLK):
            cc = pl.ds(c * BLK, BLK)
            keep = (lmask_ref[c, me] if b == 0 else pmask_ref[c, me * (n - 1) + b - 1]) > 0
            moment = moms[b, :, cc]
            square = sqs[b, :, cc]
            scaled = grads[b, :, cc] * factor
            first = jnp.where(keep, beta_one * moment + (1.0 - beta_one) * scaled, moment)
            second = jnp.where(keep, beta_two * square + (1.0 - beta_two) * scaled * scaled, square)
            update = (first * (1.0 / bias_one)) / (jnp.sqrt(second * (1.0 / bias_two)) + adam_eps)
            news[b, 0, :, cc] = first
            news[b, 1, :, cc] = second
            news[b, 2, :, cc] = jnp.where(keep, update, 0.0)
        for c in saves:
            c.start()
    gin_load.wait()
    gin_save.start()
    gin_save.wait()
    for _, saves in blocks:
        for c in saves:
            c.wait()


def adam(entries, lmask, pmask, stat, lgrad, lmom, lsq, pgrad, pmom, psq, gin):
    dma = pltpu.SemaphoreType.DMA
    vm = pl.BlockSpec(memory_space=pltpu.VMEM)
    smem = pl.BlockSpec(memory_space=pltpu.SMEM)
    hbm = pl.BlockSpec(memory_space=pl.ANY)
    rows, w = lgrad.shape
    n = 1 + pgrad.shape[0] // rows
    like = jax.ShapeDtypeStruct
    return pl.pallas_call(
        functools.partial(adam_kernel, entries=entries),
        out_shape=(like(lmom.shape, F32),) * 3
        + (like(pmom.shape, F32),) * 3
        + (like((1,) + gin.shape, F32), like((1,), F32)),
        in_specs=[smem, smem, vm] + [hbm] * 7,
        out_specs=(hbm,) * 7 + (smem,),
        scratch_shapes=[
            pltpu.VMEM(gin.shape, F32),
            pltpu.VMEM((n, rows, w), F32),
            pltpu.VMEM((n, rows, w), F32),
            pltpu.VMEM((n, rows, w), F32),
            pltpu.VMEM((n, 3, rows, w), F32),
            dma((n, 3)),
            dma((n, 3)),
            dma((2,)),
        ],
        name="adam",
    )(lmask, pmask, stat, lgrad, lmom, lsq, pgrad, pmom, psq, gin)


def per_device(
    section_input,
    out_cotangent,
    lift_weight,
    proj_weight,
    lift_mask,
    proj_mask,
    channel_perm,
    lift_moment,
    lift_square,
    proj_moment,
    proj_square,
):
    lmask, pmask = lift_mask[0].T, proj_mask[0].T
    gin, stat, lift_grad, proj_grad = token_side(
        section_input[0], out_cotangent, lift_weight[0], proj_weight[0], lmask, pmask, channel_perm
    )
    tokens = NR * NR * gin.shape[0]
    *stepped, input_grad, log_det = adam(
        tokens * lift_weight.shape[1],
        lmask,
        pmask,
        stat,
        lift_grad,
        lift_moment,
        lift_square,
        proj_grad,
        proj_moment,
        proj_square,
        gin,
    )
    return (input_grad, log_det) + tuple(stepped)


def solution(mesh):
    finer = Mesh(
        mesh.devices.reshape(NR, NR, mesh.shape["tensor"], mesh.shape["layers"]),
        ("dp_0", "dp_1", "tensor", "layers"),
    )
    tiled = P("layers", DP, "tensor")
    weight = P("layers", None, "tensor")
    return jax.shard_map(
        per_device,
        mesh=finer,
        in_specs=(tiled, P(DP, "tensor")) + (weight,) * 4 + (P("layers", None),) + (tiled,) * 4,
        out_specs=(tiled, P("layers")) + (tiled,) * 6,
        check_vma=False,
    )
```

```python
import functools

import jax
import jax.numpy as jnp
from jax import lax
from jax.experimental import pallas as pl
from jax.experimental.pallas import tpu as pltpu
from jax.sharding import Mesh
from jax.sharding import PartitionSpec as P

BLK = 128
ADAM_STEP = 10
CLIP = 4096
DP = ("dp_0", "dp_1")
MESH = pl.DeviceIdType.MESH
F32 = jnp.float32
BF16 = jnp.bfloat16

NZ = 8
NR = 4
NQ = 4

beta_one = 0.9
beta_two = 0.99
adam_eps = 1e-08


def nn(a, b):
    return jnp.dot(a, b, preferred_element_type=F32)


def nt(a, b):
    return lax.dot_general(a, b, (((1,), (1,)), ((), ())), preferred_element_type=F32)


def tn(a, b):
    return lax.dot_general(a, b, (((0,), (0,)), ((), ())), preferred_element_type=F32)


def al(i, m):
    return pl.multiple_of(i, m)


def remote(src, dst, ssem, rsem, **where):
    return pltpu.make_async_remote_copy(
        src_ref=src, dst_ref=dst, send_sem=ssem, recv_sem=rsem, device_id=where, device_id_type=MESH
    )


def far(d, h):
    return (h < NQ // 2) == (d == 0)


def both_ways(d, s, h):
    return s < 3 or far(d, h)


FIRST = [sorted(range(NQ), key=lambda h: not far(d, h)) for d in (0, 1)]
LAST = [sorted(range(NQ), key=lambda h: far(d, h)) for d in (0, 1)]


def token_kernel(
    x_ref,
    cot_ref,
    lift_hbm,
    proj_hbm,
    lmask_ref,
    pmask_ref,
    perm_ref,
    gin_out,
    stat_ref,
    lgrad_out,
    pgrad_out,
    xbuf,
    pc,
    m,
    lift,
    proj,
    cond,
    sm,
    slope,
    pre,
    stbuf,
    sbuf,
    rbuf,
    cbuf,
    c0buf,
    gbuf,
    cown,
    condc_ref,
    stc_ref,
    hid_ref,
    gp_ref,
    vec,
    zbuf,
    mid,
    pbuf,
    other,
    gin_ref,
    lgrad_ref,
    pgrad_ref,
    w_s,
    o_s,
    ag_s,
    ag_r,
    rs_s,
    rs_r,
    cs,
    cr,
    gs,
    gr,
    hs,
    hr,
    a_s,
    a_r,
    ts,
    tr,
    xs,
    xr,
    zs,
    zrv,
    ps,
    prv,
    ls,
    lr,
):
    z = lax.axis_index("tensor")
    y = lax.axis_index("dp_0")
    x = lax.axis_index("dp_1")
    core = lax.axis_index("layers")
    me = y * NR + x
    tok = x_ref.shape[0]
    half = tok // 2
    quart = tok // 4
    w = x_ref.shape[1]
    q = w // 2
    hw = NZ * q

    nq = tok // NQ

    def rows(h):
        return pl.ds(h * nq, nq)

    def zr(i):
        return lax.rem(z + NZ + i, NZ)

    zside = (zr(1), zr(-1))
    load_lift = pltpu.make_async_copy(lift_hbm, lift, w_s.at[0])
    load_proj = pltpu.make_async_copy(proj_hbm, proj, w_s.at[1])
    load_lift.start()
    load_proj.start()

    bar = pltpu.get_barrier_semaphore()
    for i in range(1, NZ):
        pl.semaphore_signal(bar, inc=1, device_id={"tensor": zr(i)}, device_id_type=MESH)
    for oy in range(NR):
        for ox in range(NR):
            if oy or ox:
                pl.semaphore_signal(
                    bar,
                    inc=1,
                    device_id={"dp_0": lax.rem(y + oy, NR), "dp_1": lax.rem(x + ox, NR)},
                    device_id_type=MESH,
                )
    pl.semaphore_signal(bar, inc=1, device_id={"layers": 1 - core}, device_id_type=MESH)

    def ag_copy(p, buf, own, s, d, h):
        origin = zr(-s) if d == 0 else zr(s)
        src = own.at[rows(h)] if s == 0 else buf.at[origin, rows(h)]
        return remote(src, buf.at[origin, rows(h)], ag_s, ag_r.at[d, s, h], tensor=zside[d])

    def ag_wait(p, buf, s, d, h):
        origin = zr(-1 - s) if d == 0 else zr(1 + s)
        ref = buf.at[origin, rows(h)]
        remote(ref, ref, ag_s, ag_r.at[d, s, h], tensor=zside[d]).wait_recv()

    def ag_start(p, buf, own):
        for k in range(NQ):
            for d in (0, 1):
                ag_copy(p, buf, own, 0, d, FIRST[d][k]).start()

    def ag_step(p, buf, own, s):
        for k in range(NQ):
            for d in (0, 1):
                h = FIRST[d][k]
                if both_ways(d, s, h):
                    ag_wait(p, buf, s, d, h)
                    if s < 3 and both_ways(d, s + 1, h):
                        ag_copy(p, buf, own, s + 1, d, h).start()
        return [zr(-1 - s), zr(1 + s)] if s < 3 else [zr(4)]

    def ring_sent(ssem, rsem):
        ref = xbuf.at[pl.ds(0, NZ - 1)]
        remote(ref, ref, ssem, rsem.at[0, 0, 0], tensor=zside[0]).wait_send()

    def rs_copy(p, s, d, h):
        return remote(
            sbuf.at[p, d, s, rows(h)],
            rbuf.at[p, d, s, rows(h)],
            rs_s,
            rs_r.at[d, s, h],
            tensor=zside[d],
        )

    def rs(p, part, tick):
        most = part(zr(4))
        for k in range(NQ // 2):
            for d in (0, 1):
                h = FIRST[d][k]
                sbuf[p, d, 0, rows(h)] = most[h * nq : (h + 1) * nq].astype(BF16)
                rs_copy(p, 0, d, h).start()
        for s in (1, 2, 3):
            mine = [part(zr(4 - s)), part(zr(s - 4))]

            def send(d, h, own):
                sbuf[p, d, s, rows(h)] = own.astype(BF16)
                rs_copy(p, s, d, h).start()

            if s == 1:
                for k in range(NQ // 2):
                    for d in (0, 1):
                        h = LAST[d][k]
                        send(d, h, mine[d][h * nq : (h + 1) * nq])
            with jax.named_scope(f"tick{s}"):
                tick(s)
            with jax.named_scope(f"w{s}"):
                for k in range(NQ // 2 if s == 1 else 0, NQ):
                    for d in (0, 1):
                        h = LAST[d][k]
                        rs_copy(p, s - 1, d, h).wait_recv()
                        own = mine[d][h * nq : (h + 1) * nq]
                        send(d, h, own + rbuf[p, d, s - 1, rows(h)].astype(F32))

        def end():
            own = part(z)
            with jax.named_scope("w4"):
                for d in (0, 1):
                    for h in range(NQ):
                        rs_copy(p, 3, d, h).wait_recv()
            return own + rbuf[p, 0, 3].astype(F32) + rbuf[p, 1, 3].astype(F32)

        return end

    def along(axis, i):
        if axis == "dp_1":
            return {"dp_1": lax.rem(x + NR + i, NR)}
        return {"dp_0": lax.rem(y + NR + i, NR)}

    def slot(buf, stage, h, off, r):
        axis = ("dp_1", "dp_0")[(h + stage) % 2]
        yy, xx = (y, lax.rem(x + NR + off, NR)) if axis == "dp_1" else (lax.rem(y + NR + off, NR), x)
        if stage == 0:
            return buf.at[yy, xx, r]
        return buf.at[yy, :, r] if axis == "dp_0" else buf.at[:, xx, r]

    def xy_rows(h, t, d):
        if t == 0:
            return pl.ds(h * half, half)
        return pl.ds(h * half + d * quart, quart)

    def xy_copy(p, buf, stage, h, t, d):
        axis = ("dp_1", "dp_0")[(h + stage) % 2]
        step = 1 if d == 0 else -1
        off = 0 if t == 0 else -step
        rr = xy_rows(h, t, d)
        if stage == 0 and t == 1:
            step, off, rr = 2, 0, xy_rows(h, 0, 0)
        src = slot(buf, stage, h, off, rr)
        return remote(src, src, xs.at[p], xr.at[p, stage, h, t, d], **along(axis, step))

    def xy_wait(p, buf, stage, h, t, d):
        step = 1 if d == 0 else -1
        off = -step if t == 0 else -2 * step
        rr = xy_rows(h, 0 if stage == 0 else t, d)
        ref = slot(buf, stage, h, off, rr)
        remote(ref, ref, xs.at[p], xr.at[p, stage, h, t, d], tensor=zside[0]).wait_recv()

    def xy_each(stage, t, act_on):
        for h in (0, 1):
            for d in (0,) if stage == 0 and t == 1 else (0, 1):
                act_on(stage, h, t, d)

    def xy_tick(p, buf, k):
        with jax.named_scope(f"xy{p}{k}"):
            for stage, t in ((), ((0, 0), (0, 1)), ((1, 0),), ((1, 1),))[k]:
                xy_each(stage, t, lambda *a: xy_wait(p, buf, *a))
            for stage, t in (((0, 0), (0, 1)), ((1, 0),), ((1, 1),), ())[k]:
                xy_each(stage, t, lambda *a: xy_copy(p, buf, *a).start())

    def xy_finish(p):
        ref = m.at[pl.ds(0, (NR * NR - 1) * tok // 2)]
        remote(ref, ref, xs.at[p], xr.at[p, 0, 0, 0, 0], tensor=zside[0]).wait_send()

    def mask_lift(i, _):
        r = pl.ds(al(i * BLK, BLK), BLK)
        for c in range(w // BLK):
            cc = pl.ds(c * BLK, BLK)
            keep = lmask_ref[c, i].astype(F32)
            lift[r, cc] = (lift[r, cc].astype(F32) * keep).astype(BF16)
        return 0

    def mask_proj(i, _):
        r = pl.ds(al(i * BLK, BLK), BLK)
        for c in range(w // BLK):
            cc = pl.ds(c * BLK, BLK)
            keep = pmask_ref[c, i].astype(F32)
            proj[r, cc] = (proj[r, cc].astype(F32) * keep).astype(BF16)
        return 0

    ca_perm = pl.ds(al(z * q, q), q)
    mv_perm = pl.ds(al(hw + z * q, q), q)

    def hot(base, order):
        at = lax.broadcasted_iota(jnp.int32, (BLK, q), 0) + base
        return jnp.where(at == order, 1.0, 0.0).astype(BF16)

    def build(i, _):
        base = i * BLK
        r = pl.ds(al(base, BLK), BLK)
        for c in range(hw // q):
            cc = pl.ds(c * q, q)
            pc[r, cc] = hot(base, perm_ref[:, cc])
        m[r, pl.ds(w, q)] = hot(base, perm_ref[:, ca_perm])
        m[r, pl.ds(w + q, q)] = hot(base, perm_ref[:, mv_perm])
        return 0

    def of(origin):
        return pl.ds(al(origin * w, w), w)

    def spread(origin):
        with jax.named_scope("spread"):
            m[of(origin), pl.ds(0, w)] = nn(pc[of(origin), :], lift[...]).astype(BF16)

    def times(origin):
        return nn(xbuf[origin], m[of(origin), pl.ds(0, w)])

    def pick(c, _):
        cc = pl.ds(al(c * q, q), q)
        got = nn(xbuf[0], pc[pl.ds(0, w), cc])
        for o in range(1, NZ):
            got = got + nn(xbuf[o], pc[pl.ds(o * w, w), cc])
        cond[:, cc] = got.astype(BF16)
        return 0

    with jax.named_scope("build"):
        lax.fori_loop(0, 2 * hw // BLK, build, 0)
    xbuf[z] = x_ref[...]
    load_lift.wait()
    lax.fori_loop(0, hw // BLK, mask_lift, 0)
    spread(z)
    spread(zr(-1))
    with jax.named_scope("barrier"):
        pl.semaphore_wait(bar, NZ - 1 + NR * NR - 1 + 1)
    ag_start(0, xbuf, x_ref)

    @pl.when(core == 1)
    def _():
        for e in (0, 1):
            dest = lax.rem(2 * z + e, NZ)
            piece = cot_ref.at[:, pl.ds(e * q, q)]
            land = cbuf.at[:, pl.ds(al((z // 4) * q, q), q)]

            @pl.when(dest != z)
            def _():
                remote(piece, land, cs.at[e], cr.at[z // 4], tensor=dest).start()

            @pl.when(dest == z)
            def _():
                cbuf[:, pl.ds(al((z // 4) * q, q), q)] = cot_ref[:, pl.ds(e * q, q)]

    spread(zr(1))
    pre[...] = times(z)
    spread(zr(-2))
    spread(zr(2))
    load_proj.wait()
    with jax.named_scope("mask_proj"):
        lax.fori_loop(0, 2 * hw // BLK, mask_proj, 0)
    for s in range(4):
        with jax.named_scope(f"agx{s}"):
            came = ag_step(0, xbuf, x_ref, s)
        if s < 3:
            spread((zr(-3), zr(3), zr(4))[s])
        for origin in came:
            pre[...] += times(origin)

    ring_sent(ag_s, ag_r)

    squash = jax.nn.sigmoid(pre[...])
    slope[...] = squash * (1.0 + pre[...] * (1.0 - squash))
    hid_ref[y, x] = (pre[...] * squash).astype(BF16)
    xy_tick(0, hid_ref, 0)

    hidden = hid_ref[y, x]

    def proj_rows(d, k):
        return pl.ds(al(k * hw + d * q, q), q)

    def shared_part(d):
        return jnp.concatenate(
            [nt(hidden, proj[proj_rows(d, 0), :]), nt(hidden, proj[proj_rows(d, 1), :])], axis=1
        )

    def shared_tick(s):
        if s == 1:
            got = nn(xbuf[0], m[pl.ds(0, w), pl.ds(w + q, q)])
            for o in range(1, NZ):
                got = got + nn(xbuf[o], m[pl.ds(o * w, w), pl.ds(w + q, q)])
            sm[:, pl.ds(q, q)] = got

    with jax.named_scope("rs_shared"):
        shared = rs(0, shared_part, shared_tick)()
    ring_sent(rs_s, rs_r)
    raw = shared[:, :q] + 2.0
    scale = jax.nn.sigmoid(raw)
    sm[:, pl.ds(0, q)] = scale
    sm[:, pl.ds(q, q)] += shared[:, q:]
    logs = jnp.minimum(raw, 0.0) - jnp.log1p(jnp.exp(-jnp.abs(raw)))
    logs = jnp.sum(logs.reshape(tok // 8, 8, q), axis=0)
    vec[1] = logs[:, :BLK] + logs[:, BLK:]
    xy_tick(0, hid_ref, 1)

    def cond_copy(o):
        oy, ox = o // NR, o % NR
        ty, tx = lax.rem(y + oy, NR), lax.rem(x + ox, NR)
        return remote(
            cond.at[:, pl.ds(al((ty * NR + tx) * BLK, BLK), BLK)],
            condc_ref.at[me],
            a_s,
            a_r,
            dp_0=ty,
            dp_1=tx,
        )

    def all_of(buf, ssem, rsem):
        ref = buf.at[pl.ds(0, buf.shape[0] - 1)]
        return remote(ref, ref, ssem, rsem, dp_0=lax.rem(y + 1, NR))

    def permute_tokens(lo, hi):
        with jax.named_scope("permute"):
            lax.fori_loop(lo, hi, pick, 0)
        if hi == hw // q:
            for o in range(1, NR * NR):
                cond_copy(o).start()
            condc_ref[me] = cond[:, pl.ds(al(me * BLK, BLK), BLK)]

    @pl.when(core == 1)
    def _():
        for k in (0, 1):

            @pl.when(4 * k + z // 2 != z)
            def _():
                ref = cbuf.at[:, pl.ds(k * q, q)]
                remote(ref, ref, cs.at[0], cr.at[k], tensor=z).wait_recv()

        cown[...] = cbuf[...]

    @pl.when(core == 0)
    def _():
        permute_tokens(0, hw // q)
        with jax.named_scope("handwait"):
            remote(gbuf, c0buf, hs, hr, layers=1 - core).wait_recv()
        cown[...] = c0buf[...]

    ca = cown[:, pl.ds(0, q)]
    cb = cown[:, pl.ds(q, q)].astype(F32)
    scale = sm[:, pl.ds(0, q)]
    keep_part = 1.0 - scale
    shift_grad = (cb * scale).astype(BF16)
    raw_grad = (cb * sm[:, pl.ds(q, q)] * scale * keep_part - keep_part).astype(BF16)
    stbuf[z, :, pl.ds(0, q)] = raw_grad
    stbuf[z, :, pl.ds(q, q)] = shift_grad
    own_st = stbuf.at[z]
    ag_start(1, stbuf, own_st)

    def st_copy(origin, k):
        to = origin + NZ * k
        return remote(
            stbuf.at[origin, :, pl.ds(k * q, q)],
            stc_ref.at[me],
            ts,
            tr,
            dp_0=to // NR,
            dp_1=lax.rem(to, NR),
        )

    def st_send(origin):
        for k in (0, 1):

            @pl.when(origin + NZ * k != me)
            def _():
                st_copy(origin, k).start()

            @pl.when(origin + NZ * k == me)
            def _():
                stc_ref[me] = stbuf[origin, :, pl.ds(k * q, q)]

    def act(origin):
        return nn(stbuf[origin, :, pl.ds(0, q)], proj[proj_rows(origin, 0), :]) + nn(
            stbuf[origin, :, pl.ds(q, q)], proj[proj_rows(origin, 1), :]
        )

    pre[...] = act(z)
    st_send(z)

    @pl.when(core == 1)
    def _():
        permute_tokens(0, 5)

    for s in range(4):
        with jax.named_scope(f"agst{s}"):
            came = ag_step(1, stbuf, own_st, s)
        if s < 2:
            for origin in came:
                st_send(origin)
        for origin in came:
            pre[...] += act(origin)
        if s == 0:

            @pl.when(core == 1)
            def _():
                permute_tokens(5, hw // q)

        if s == 0:

            @pl.when(core == 0)
            def _():
                xy_tick(0, hid_ref, 2)

        if s == 2:

            @pl.when(core == 1)
            def _():
                xy_tick(0, hid_ref, 2)

    grad_pre = (pre[...] * slope[...]).astype(BF16)
    gp_ref[y, x] = grad_pre
    xy_tick(1, gp_ref, 0)

    lhs = jnp.concatenate([grad_pre, ca, shift_grad], axis=1)

    def in_rows(d, k):
        there = jnp.where(core == 1, k * hw + d * q, (2 * d + k) * q)
        return pl.ds(al(there, q), q)

    def in_part(d):
        return jnp.concatenate([nt(lhs, m[in_rows(d, 0), :]), nt(lhs, m[in_rows(d, 1), :])], axis=1)

    def in_tick(s):
        if s != 2:

            @pl.when(core == 0)
            def _():
                xy_tick(1, gp_ref, (s + 1) // 2)

        if s == 1:
            for i in (-3, 3, 4):
                st_send(zr(i))

    with jax.named_scope("rs_in"):
        end = rs(1, in_part, in_tick)

    def gsend(k):
        return remote(
            cown.at[:, pl.ds(k * q, q)],
            gbuf.at[:, pl.ds(al(lax.rem(z, 2) * q, q), q)],
            gs.at[k],
            gr.at[lax.rem(z, 2)],
            tensor=4 * k + z // 2,
        )

    @pl.when(core == 1)
    def _():
        cown[...] = end().astype(BF16)
        remote(cown, c0buf, hs, hr, layers=1 - core).start()
        for k in (0, 1):

            @pl.when(4 * k + z // 2 != z)
            def _():
                gsend(k).start()

            @pl.when(4 * k + z // 2 == z)
            def _():
                gbuf[:, pl.ds(al(lax.rem(z, 2) * q, q), q)] = cown[:, pl.ds(k * q, q)]

        xy_tick(1, gp_ref, 1)
        xy_tick(0, hid_ref, 3)
        xy_tick(1, gp_ref, 2)

    tokens = NR * NR * tok

    def squares(g):
        g = jnp.sum((g * g).reshape(g.shape[0] // 8, 8, w), axis=0)
        out = g[:, :BLK]
        for c in range(1, w // BLK):
            out = out + g[:, c * BLK : (c + 1) * BLK]
        return out

    @pl.when(core == 0)
    def _():
        xy_tick(0, hid_ref, 3)

    with jax.named_scope("stcome"):
        all_of(stc_ref, ts, tr).wait_recv()
    with jax.named_scope("pgrad"):
        pgrad_ref[...] = tn(stc_ref[...].reshape(tokens, q), hid_ref[...].reshape(tokens, w))
    for b in range(q // BLK):
        for c in range(w // BLK):
            keep = pmask_ref[c, me * (q // BLK) + b].astype(F32)
            pgrad_ref[pl.ds(b * BLK, BLK), pl.ds(c * BLK, BLK)] *= keep
    vec[0] = squares(pgrad_ref[...])
    with jax.named_scope("condwait"):
        all_of(condc_ref, a_s, a_r).wait_recv()
    xy_tick(1, gp_ref, 3)
    with jax.named_scope("lgrad"):
        lgrad_ref[...] = tn(condc_ref[...].reshape(tokens, BLK), gp_ref[...].reshape(tokens, w))
    for c in range(w // BLK):
        keep = lmask_ref[c, me].astype(F32)
        lgrad_ref[:, pl.ds(c * BLK, BLK)] *= keep
    vec[0] += squares(lgrad_ref[...])

    save_pgrad = pltpu.make_async_copy(pgrad_ref, pgrad_out, o_s.at[0])
    save_lgrad = pltpu.make_async_copy(lgrad_ref, lgrad_out, o_s.at[1])
    save_gin = pltpu.make_async_copy(gin_ref, gin_out, o_s.at[2])
    def zcopy(i):
        return remote(vec, zbuf.at[z], zs, zrv, tensor=zr(i))

    for i in range(1, NZ):
        zcopy(i).start()
    zbuf[z] = vec[...]
    save_pgrad.start()
    save_lgrad.start()

    @pl.when(core == 1)
    def _():
        for e in (0, 1):

            @pl.when(lax.rem(2 * z + e, NZ) != z)
            def _():
                ref = gbuf.at[:, pl.ds(e * q, q)]
                remote(ref, ref, gs.at[0], gr.at[e], tensor=z).wait_recv()

        gin_ref[...] = gbuf[...].astype(F32)

    @pl.when(core == 0)
    def _():
        gin_ref[...] = end()

    save_gin.start()
    with jax.named_scope("zsum"):
        all_of(zbuf, zs, zrv).wait_recv()
    mid[...] = jnp.sum(zbuf[...], axis=0)

    def pcopy(o):
        ty, tx = lax.rem(y + o // NR, NR), lax.rem(x + o % NR, NR)
        return remote(mid, pbuf.at[me], ps, prv, dp_0=ty, dp_1=tx)

    for o in range(1, NR * NR):
        pcopy(o).start()
    pbuf[me] = mid[...]
    @pl.when(core == 1)
    def _():
        remote(cown, c0buf, hs, hr, layers=1 - core).wait_send()
        for k in (0, 1):

            @pl.when(4 * k + z // 2 != z)
            def _():
                gsend(k).wait_send()

        for e in (0, 1):
            dest = lax.rem(2 * z + e, NZ)

            @pl.when(dest != z)
            def _():
                ref = cot_ref.at[:, pl.ds(e * q, q)]
                remote(ref, ref, cs.at[e], cr.at[0], tensor=dest).wait_send()

    all_of(condc_ref, a_s, a_r).wait_send()
    all_of(stc_ref, ts, tr).wait_send()
    ring_sent(ag_s, ag_r)
    ring_sent(rs_s, rs_r)
    xy_finish(0)
    xy_finish(1)
    save_pgrad.wait()
    save_lgrad.wait()
    save_gin.wait()
    all_of(zbuf, zs, zrv).wait_send()

    with jax.named_scope("psum"):
        all_of(pbuf, ps, prv).wait_recv()
    other[0] = jnp.sum(pbuf[...], axis=0)
    swap = remote(other.at[0], other.at[1], ls, lr, layers=1 - core)
    swap.start()

    all_of(pbuf, ps, prv).wait_send()
    with jax.named_scope("swap"):
        swap.wait_recv()
    stat_ref[0] = other[0, 0] + other[1, 0]
    stat_ref[1] = other[0, 1]
    swap.wait_send()


def token_side(x, cot, lift_w, proj_w, lmask, pmask, perm):
    tok, w = x.shape
    hw = lift_w.shape[0]
    feat = 2 * hw
    q = w // 2
    dma = pltpu.SemaphoreType.DMA
    vm = pl.BlockSpec(memory_space=pltpu.VMEM)
    sm = pl.BlockSpec(memory_space=pltpu.SMEM)
    hbm = pl.BlockSpec(memory_space=pl.ANY)
    n = NR * NR
    return pl.pallas_call(
        token_kernel,
        out_shape=(
            jax.ShapeDtypeStruct((tok, w), F32),
            jax.ShapeDtypeStruct((2, 8, BLK), F32),
            jax.ShapeDtypeStruct((BLK, w), F32),
            jax.ShapeDtypeStruct((q, w), F32),
        ),
        in_specs=[vm, vm, hbm, hbm, sm, sm, vm],
        out_specs=(hbm, vm, hbm, hbm),
        scratch_shapes=[
            pltpu.VMEM((NZ, tok, w), BF16),
            pltpu.VMEM((feat, hw), BF16),
            pltpu.VMEM((feat, 2 * w), BF16),
            pltpu.VMEM((hw, w), BF16),
            pltpu.VMEM((feat, w), BF16),
            pltpu.VMEM((tok, hw), BF16),
            pltpu.VMEM((tok, w), F32),
            pltpu.VMEM((tok, w), F32),
            pltpu.VMEM((tok, w), F32),
            pltpu.VMEM((NZ, tok, w), BF16),
            pltpu.VMEM((2, 2, 4, tok, w), BF16),
            pltpu.VMEM((2, 2, 4, tok, w), BF16),
            pltpu.VMEM((tok, w), BF16),
            pltpu.VMEM((tok, w), BF16),
            pltpu.VMEM((tok, w), BF16),
            pltpu.VMEM((tok, w), BF16),
            pltpu.VMEM((n, tok, BLK), BF16),
            pltpu.VMEM((n, tok, q), BF16),
            pltpu.VMEM((NR, NR, tok, w), BF16),
            pltpu.VMEM((NR, NR, tok, w), BF16),
            pltpu.VMEM((2, 8, BLK), F32),
            pltpu.VMEM((NZ, 2, 8, BLK), F32),
            pltpu.VMEM((2, 8, BLK), F32),
            pltpu.VMEM((n, 2, 8, BLK), F32),
            pltpu.VMEM((2, 2, 8, BLK), F32),
            pltpu.VMEM((tok, w), F32),
            pltpu.VMEM((BLK, w), F32),
            pltpu.VMEM((q, w), F32),
            dma((2,)),
            dma((3,)),
            dma,
            dma((2, 4, NQ)),
            dma,
            dma((2, 4, NQ)),
            dma((2,)),
            dma((2,)),
            dma((2,)),
            dma((2,)),
            dma,
            dma,
            dma,
            dma,
            dma,
            dma,
            dma((2,)),
            dma((2, 2, 2, 2, 2)),
            dma,
            dma,
            dma,
            dma,
            dma,
            dma,
        ],
        compiler_params=pltpu.CompilerParams(
            collective_id=0, has_side_effects=True, vmem_limit_bytes=64 * 1024 * 1024 - 64 * 1024
        ),
        name="token_side",
    )(x, cot, lift_w, proj_w, lmask, pmask, perm)


def adam_kernel(
    lmask_ref,
    pmask_ref,
    stat_ref,
    lgrad_hbm,
    lmom_hbm,
    lsq_hbm,
    pgrad_hbm,
    pmom_hbm,
    psq_hbm,
    gin_hbm,
    lfirst_out,
    lsecond_out,
    lupdate_out,
    pfirst_out,
    psecond_out,
    pupdate_out,
    gin_out,
    log_ref,
    gin,
    grads,
    moms,
    sqs,
    news,
    in_s,
    out_s,
    gin_s,
    *,
    entries,
):
    me = lax.axis_index("dp_0") * NR + lax.axis_index("dp_1")
    n, rows, w = grads.shape
    per = BLK // rows
    blocks = []
    for b in range(n):
        r = pl.ds((b if b < per else b - per) * rows, rows)
        if b < per:
            ins = [lgrad_hbm.at[r], lmom_hbm.at[0, r], lsq_hbm.at[0, r]]
            outs = [lfirst_out.at[0, r], lsecond_out.at[0, r], lupdate_out.at[0, r]]
        else:
            ins = [pgrad_hbm.at[r], pmom_hbm.at[0, r], psq_hbm.at[0, r]]
            outs = [pfirst_out.at[0, r], psecond_out.at[0, r], pupdate_out.at[0, r]]
        loads = [
            pltpu.make_async_copy(ref, buf.at[b], in_s.at[b, k])
            for k, (ref, buf) in enumerate(zip(ins, (grads, moms, sqs)))
        ]
        saves = [pltpu.make_async_copy(news.at[b, k], ref, out_s.at[b, k]) for k, ref in enumerate(outs)]
        blocks.append((loads, saves))
    for loads, _ in blocks:
        for c in loads:
            c.start()
    gin_load = pltpu.make_async_copy(gin_hbm, gin, gin_s.at[0])
    gin_save = pltpu.make_async_copy(gin, gin_out.at[0], gin_s.at[1])
    gin_load.start()
    total = jnp.sum(stat_ref[0], keepdims=True)
    factor = jnp.minimum(1.0, CLIP / (jnp.sqrt(total) + 1e-06))
    log_ref[0] = jnp.sum(stat_ref[1]) * (1.0 / entries)
    bias_one = 1.0 - beta_one**ADAM_STEP
    bias_two = 1.0 - beta_two**ADAM_STEP
    for b, (loads, saves) in enumerate(blocks):
        for c in loads:
            c.wait()
        for c in range(w // BLK):
            cc = pl.ds(c * BLK, BLK)
            keep = (lmask_ref[c, me] if b < per else pmask_ref[c, me * (n // per - 1) + b // per - 1]) > 0
            moment = moms[b, :, cc]
            square = sqs[b, :, cc]
            scaled = grads[b, :, cc] * factor
            first = jnp.where(keep, beta_one * moment + (1.0 - beta_one) * scaled, moment)
            second = jnp.where(keep, beta_two * square + (1.0 - beta_two) * scaled * scaled, square)
            update = (first * (1.0 / bias_one)) / (jnp.sqrt(second * (1.0 / bias_two)) + adam_eps)
            news[b, 0, :, cc] = first
            news[b, 1, :, cc] = second
            news[b, 2, :, cc] = jnp.where(keep, update, 0.0)
        for c in saves:
            c.start()
    gin_load.wait()
    gin_save.start()
    gin_save.wait()
    for _, saves in blocks:
        for c in saves:
            c.wait()


def adam(entries, lmask, pmask, stat, lgrad, lmom, lsq, pgrad, pmom, psq, gin):
    dma = pltpu.SemaphoreType.DMA
    vm = pl.BlockSpec(memory_space=pltpu.VMEM)
    smem = pl.BlockSpec(memory_space=pltpu.SMEM)
    hbm = pl.BlockSpec(memory_space=pl.ANY)
    rows, w = BLK // 2, lgrad.shape[1]
    n = (lgrad.shape[0] + pgrad.shape[0]) // rows
    like = jax.ShapeDtypeStruct
    return pl.pallas_call(
        functools.partial(adam_kernel, entries=entries),
        out_shape=(like(lmom.shape, F32),) * 3
        + (like(pmom.shape, F32),) * 3
        + (like((1,) + gin.shape, F32), like((1,), F32)),
        in_specs=[smem, smem, vm] + [hbm] * 7,
        out_specs=(hbm,) * 7 + (smem,),
        scratch_shapes=[
            pltpu.VMEM(gin.shape, F32),
            pltpu.VMEM((n, rows, w), F32),
            pltpu.VMEM((n, rows, w), F32),
            pltpu.VMEM((n, rows, w), F32),
            pltpu.VMEM((n, 3, rows, w), F32),
            dma((n, 3)),
            dma((n, 3)),
            dma((2,)),
        ],
        name="adam",
    )(lmask, pmask, stat, lgrad, lmom, lsq, pgrad, pmom, psq, gin)


def per_device(
    section_input,
    out_cotangent,
    lift_weight,
    proj_weight,
    lift_mask,
    proj_mask,
    channel_perm,
    lift_moment,
    lift_square,
    proj_moment,
    proj_square,
):
    lmask, pmask = lift_mask[0].T, proj_mask[0].T
    gin, stat, lift_grad, proj_grad = token_side(
        section_input[0], out_cotangent, lift_weight[0], proj_weight[0], lmask, pmask, channel_perm
    )
    tokens = NR * NR * gin.shape[0]
    *stepped, input_grad, log_det = adam(
        tokens * lift_weight.shape[1],
        lmask,
        pmask,
        stat,
        lift_grad,
        lift_moment,
        lift_square,
        proj_grad,
        proj_moment,
        proj_square,
        gin,
    )
    return (input_grad, log_det) + tuple(stepped)


def solution(mesh):
    finer = Mesh(
        mesh.devices.reshape(NR, NR, mesh.shape["tensor"], mesh.shape["layers"]),
        ("dp_0", "dp_1", "tensor", "layers"),
    )
    tiled = P("layers", DP, "tensor")
    weight = P("layers", None, "tensor")
    return jax.shard_map(
        per_device,
        mesh=finer,
        in_specs=(tiled, P(DP, "tensor")) + (weight,) * 4 + (P("layers", None),) + (tiled,) * 4,
        out_specs=(tiled, P("layers")) + (tiled,) * 6,
        check_vma=False,
    )
```
